32 devices in a mesh: wide: 8 (over y, x, core), narrow: 4 (over z).
Axes of the slice: x: 2, y: 2, z: 4, core: 2. Of those that a mesh axis runs over, the one named last changes fastest.
Arguments:
- amplitudes: float32 [2, 8, 8, 4, 128, 128], P(None, None, 'wide', 'narrow'), may hold values from -6 to 6
- gates: float32 [3, 2, 2, 128, 128], replicated, may hold values from -0.375 to 0.375
Outputs:
- final_state: float32 [2, 8, 8, 4, 128, 128], P(None, None, 'wide', 'narrow')
The draws below stay inside these ranges and needn't reach their ends.
All inputs are finite; a program needn't handle non-finite values.
Results may differ from the reference program's by a relative error of at most 0.0001.
Values sent between devices are 32-bit elements; how exact they have to be, the bound alone decides.
A program may use at most 64 MiB of HBM per device.

```python
import jax
import jax.numpy as jnp
from jax import lax

ORDER = 128
SLABS = 8
N_WIDE = 8
N_NARROW = 4


def shard_levels(rng, dims, split, smallest, high):
    level = 1.0
    for dim, blocks in split:
        heights = jax.random.uniform(jax.random.fold_in(jax.random.fold_in(rng, 6), dim), (blocks,), jnp.float32, smallest / len(split), high / len(split))
        level = level * jnp.repeat(jnp.exp(heights), dims[dim] // blocks).reshape((-1,) + (1,) * (len(dims) - 1 - dim))
    return level


def scatter_about(key, dims, spread, most, split=(), dtype=jnp.bfloat16):
    gain = shard_levels(key, dims, split, -0.22, 0.18) if split else 1.0
    array = jax.random.normal(key, dims, jnp.float32) * spread * gain
    return jnp.minimum(jnp.maximum(array, -most), most).astype(dtype)


def setup_inputs(seed: int = 0) -> dict:
    key_list = jax.random.split(jax.random.key(seed), 3)
    amplitudes = scatter_about(key_list[0], (2, SLABS, N_WIDE, N_NARROW, ORDER, ORDER), 1.0, 6.0, ((2, 8), (3, 4)), jnp.float32)
    gates = scatter_about(key_list[1], (3, 2, 2, ORDER, ORDER), (2 * ORDER) ** -0.5, 0.375, (), jnp.float32)
    return {"amplitudes": amplitudes, "gates": gates}


def blocks(matrix):
    return jnp.stack([jnp.stack([matrix[0], -matrix[1]]), jnp.stack([matrix[1], matrix[0]])])


def on_rows(vector, matrix):
    return jnp.einsum("cdjk,drwnkb->crwnjb", blocks(matrix), vector, precision=lax.Precision.HIGHEST)


def on_columns(vector, matrix):
    return jnp.einsum("cdjk,drwnak->crwnaj", blocks(matrix), vector, precision=lax.Precision.HIGHEST)


def reference(amplitudes, gates):
    vector = amplitudes
    layout = amplitudes.shape
    for section_index in range(3):
        vector = on_rows(vector, gates[section_index, 0])
        vector = on_columns(vector, gates[section_index, 1])
        if section_index == 0:
            split_size = ORDER // N_WIDE
            vector = vector.reshape(2, SLABS, N_WIDE, N_NARROW, N_WIDE, split_size, ORDER)
            vector = vector.transpose(0, 1, 4, 3, 2, 5, 6).reshape(layout)
        if section_index == 1:
            split_size = ORDER // N_NARROW
            vector = vector.reshape(2, SLABS, N_WIDE, N_NARROW, N_NARROW, split_size, ORDER)
            vector = vector.transpose(0, 1, 2, 4, 3, 5, 6).reshape(layout)
    return vector
```

```python
import functools

import jax
import jax.numpy as jnp
from jax import lax
from jax.experimental import pallas as pl
from jax.experimental.pallas import tpu as pltpu
from jax.sharding import PartitionSpec as P

precise = lax.Precision.HIGHEST
MESH = pl.DeviceIdType.MESH
F32 = jnp.float32
BF16 = jnp.bfloat16
EARLY_AT = 4
TAIL = 1


def blocks(matrix):
    return jnp.stack([jnp.stack([matrix[0], -matrix[1]]), jnp.stack([matrix[1], matrix[0]])])


def on_rows(vector, matrix):
    return jnp.einsum("cdjk,drkb->crjb", blocks(matrix), vector, precision=precise)


def on_columns(vector, matrix):
    return jnp.einsum("cdjk,drak->craj", blocks(matrix), vector, precision=precise)


def plain(amplitudes, gates):
    layout = amplitudes.shape
    slabs, order = layout[1], layout[4]
    vector = amplitudes.reshape(2, slabs, order, order)
    vector = on_columns(on_rows(vector, gates[0, 0]), gates[0, 1])
    vector = lax.all_to_all(vector.reshape(layout), "wide", split_axis=4, concat_axis=2, tiled=True)
    vector = vector.reshape(2, slabs, order, order)
    vector = on_columns(on_rows(vector, gates[1, 0]), gates[1, 1])
    vector = lax.all_to_all(vector.reshape(layout), "narrow", split_axis=4, concat_axis=3, tiled=True)
    vector = vector.reshape(2, slabs, order, order)
    vector = on_columns(on_rows(vector, gates[2, 0]), gates[2, 1])
    return vector.reshape(layout)


def partner(me, mask, count):
    out, bit = 0, 1
    while bit < count:
        digit = me // bit % 2
        if mask & bit:
            digit = 1 - digit
        out = out + digit * bit
        bit *= 2
    return out


def far_first(count):
    return sorted(range(1, count), key=lambda m: (-bin(m >> 1).count("1"), -m))


def split(value):
    high = value.astype(BF16)
    return high, (value - high.astype(F32)).astype(BF16)


def real_form(matrix):
    re, im = matrix[0], matrix[1]
    return jnp.concatenate(
        [jnp.concatenate([re, -im], axis=1), jnp.concatenate([im, re], axis=1)], axis=0
    )


def kernel(wide, narrow, early, amp, gates, out, x, g, y, yr, z, zr, left, right,
           load_sem, gate_sem, ws_sem, wr_sem, ns_sem, nr_sem, es_sem, er_sem):
    slabs, order = amp.shape[1], amp.shape[2]
    last = slabs - 1
    hw, hn = order // wide, order // narrow
    w, n = lax.axis_index("wide"), lax.axis_index("narrow")
    wide_masks = far_first(wide)
    narrow_masks = list(range(1, narrow))

    barrier = pltpu.get_barrier_semaphore()
    for mask in wide_masks:
        pl.semaphore_signal(barrier, inc=1, device_id=(partner(w, mask, wide), n), device_id_type=MESH)
    for mask in narrow_masks:
        pl.semaphore_signal(barrier, inc=1, device_id=(w, partner(n, mask, narrow)), device_id_type=MESH)

    def load(c):
        return pltpu.make_async_copy(amp.at[:, c], x.at[:, c], load_sem.at[c])

    def load_gate(t, k):
        return pltpu.make_async_copy(gates.at[t, k], g.at[t, k], gate_sem.at[t, k])

    load_gate(0, 0).start()
    if early:
        load(last).start()
    load(0).start()
    for t in range(3):
        for k in range(2):
            if (t, k) != (0, 0):
                load_gate(t, k).start()
    for c in range(1, last if early else slabs):
        load(c).start()

    def send_wide(c, i):
        there = partner(w, wide_masks[i], wide)
        return pltpu.make_async_remote_copy(
            src_ref=y.at[c, :, pl.ds(pl.multiple_of(there * hw, hw), hw), :],
            dst_ref=yr.at[c, :, pl.ds(pl.multiple_of(w * hw, hw), hw), :],
            send_sem=ws_sem.at[0], recv_sem=wr_sem.at[c],
            device_id=(there, n), device_id_type=MESH)

    def send_narrow(c, i):
        there = partner(n, narrow_masks[i], narrow)
        return pltpu.make_async_remote_copy(
            src_ref=z.at[c, :, pl.ds(pl.multiple_of(there * hn, hn), hn), :],
            dst_ref=zr.at[c, :, pl.ds(pl.multiple_of(n * hn, hn), hn), :],
            send_sem=ns_sem.at[0], recv_sem=nr_sem.at[c],
            device_id=(w, there), device_id_type=MESH)

    def send_early():
        return pltpu.make_async_remote_copy(
            src_ref=x.at[:, last], dst_ref=x.at[:, slabs],
            send_sem=es_sem.at[0], recv_sem=er_sem.at[0],
            device_id=(w, partner(n, 3, narrow)), device_id_type=MESH)

    def send_half(k):
        there = partner(n, 1, narrow)
        index = partner(n, 3 * k, narrow)
        return pltpu.make_async_remote_copy(
            src_ref=z.at[last + k, :, pl.ds(pl.multiple_of(there * hn, hn), hn), :],
            dst_ref=zr.at[last, :, pl.ds(pl.multiple_of(index * hn, hn), hn), :],
            send_sem=es_sem.at[1 + k], recv_sem=er_sem.at[1 + k],
            device_id=(w, there), device_id_type=MESH)

    def arrived(ref, sem):
        pltpu.make_async_copy(ref, ref, sem).wait()

    def prepare(t):
        load_gate(t, 0).wait()
        high, low = split(real_form(g[t, 0]))
        left[t] = jnp.concatenate([high, low, high], axis=1)

    def rows(t, value):
        high, low = split(value.reshape(2 * order, order))
        stacked = jnp.concatenate([high, high, low], axis=0)
        return jnp.dot(left[t], stacked, preferred_element_type=F32)

    def columns(value):
        high, low = split(jnp.concatenate([value[:order], value[order:]], axis=1))
        stacked = jnp.concatenate([high, low, high], axis=1)
        return jnp.dot(stacked, right[...], preferred_element_type=F32)

    def first(c, loaded=False):
        if not loaded:
            load(c).wait()
        y[c] = rows(0, x[:, c]).reshape(2, order, order)

    def start_wide(c):
        for i in range(wide - 1):
            send_wide(c, i).start()

    prepare(0)
    first(0)
    if early:
        load(last).wait()
    pl.semaphore_wait(barrier, wide + narrow - 2)
    if early:
        send_early().start()
    start_wide(0)
    prepare(1)

    @pl.loop(1, last if early else slabs)
    def _(c):
        first(c)
        start_wide(c)

    if early:
        first(last, True)
        start_wide(last)

    def second(c, with_columns, with_narrow=True):
        own = pl.ds(pl.multiple_of(w * hw, hw), hw)
        yr[c, :, own, :] = y[c, :, own, :]
        arrived(yr.at[c, :, pl.ds(0, hw * (wide - 1)), :], wr_sem.at[c])
        value = rows(1, yr[c])
        if with_columns:
            value = columns(value)
            z[c, 0] = value[:, :order]
            z[c, 1] = value[:, order:]
        else:
            z[c] = value.reshape(2, order, order)
        if not with_narrow:
            return
        for i in range(narrow - 1):
            send_narrow(c, i).start()

    second(0, False)

    for t in range(3):
        load_gate(t, 1).wait()
    product = g[0, 1].reshape(2 * order, order)
    for t in (1, 2):
        product = jnp.dot(real_form(g[t, 1]), product, precision=precise, preferred_element_type=F32)
    re, im = product[:order].T, product[order:].T
    high, low = split(jnp.concatenate(
        [jnp.concatenate([re, im], axis=1), jnp.concatenate([-im, re], axis=1)], axis=0))
    right[...] = jnp.concatenate([high, high, low], axis=0)
    prepare(2)

    if early:
        @pl.loop(1, EARLY_AT)
        def _(c):
            second(c, True)

        send_early().wait_recv()
        first(slabs, True)
        start_wide(slabs)

        @pl.loop(EARLY_AT, last - TAIL)
        def _(c):
            second(c, True)

        @pl.loop(last, slabs + 1)
        def _(c):
            second(c, False, False)

        for k in range(2):
            send_half(k).start()
            index = partner(n, 3 * k, narrow)
            rows_to = pl.ds(pl.multiple_of(index * hn, hn), hn)
            rows_from = pl.ds(pl.multiple_of(n * hn, hn), hn)
            zr[last, :, rows_to, :] = z[last + k, :, rows_from, :]

        @pl.loop(last - TAIL, last)
        def _(c):
            second(c, True)
    else:
        @pl.loop(1, slabs)
        def _(c):
            second(c, True)

    def third(c, with_columns, exchanged=False):
        if not exchanged:
            own = pl.ds(pl.multiple_of(n * hn, hn), hn)
            zr[c, :, own, :] = z[c, :, own, :]
            arrived(zr.at[c, :, pl.ds(0, hn * (narrow - 1)), :], nr_sem.at[c])
        value = rows(2, zr[c])
        if with_columns:
            value = columns(value)
            out[0, c] = value[:, :order]
            out[1, c] = value[:, order:]
        else:
            out[0, c] = value[:order]
            out[1, c] = value[order:]

    third(0, True)
    if early:
        @pl.loop(1, last - TAIL)
        def _(c):
            third(c, False)

        for k in range(2):
            send_half(k).wait_recv()
        third(last, True, True)

        @pl.loop(last - TAIL, last)
        def _(c):
            third(c, False)
    else:
        @pl.loop(1, slabs)
        def _(c):
            third(c, False)

    arrived(y.at[:, :, pl.ds(0, hw * (wide - 1)), :], ws_sem.at[0])
    sent = z.at[pl.ds(0, last if early else slabs), :, pl.ds(0, hn * (narrow - 1)), :]
    arrived(sent, ns_sem.at[0])

    if early:
        send_early().wait_send()
        for k in range(2):
            send_half(k).wait_send()


def fused(wide, narrow, amplitudes, gates):
    layout = amplitudes.shape
    slabs, order = layout[1], layout[4]
    vector = amplitudes.reshape(2, slabs, order, order)
    early = narrow == 4 and slabs > EARLY_AT + TAIL
    slots = slabs + early
    slab_buffer = pltpu.VMEM((slots, 2, order, order), F32)
    result = pl.pallas_call(
        functools.partial(kernel, wide, narrow, early),
        out_shape=jax.ShapeDtypeStruct(vector.shape, F32),
        in_specs=[pl.BlockSpec(memory_space=pl.ANY)] * 2,
        out_specs=pl.BlockSpec(memory_space=pltpu.VMEM),
        scratch_shapes=[
            pltpu.VMEM((2, slots, order, order), F32),
            pltpu.VMEM(gates.shape, F32),
            slab_buffer, slab_buffer, slab_buffer, slab_buffer,
            pltpu.VMEM((3, 2 * order, 6 * order), BF16),
            pltpu.VMEM((6 * order, 2 * order), BF16),
            pltpu.SemaphoreType.DMA((slabs,)),
            pltpu.SemaphoreType.DMA((3, 2)),
            pltpu.SemaphoreType.DMA((1,)),
            pltpu.SemaphoreType.DMA((slots,)),
            pltpu.SemaphoreType.DMA((1,)),
            pltpu.SemaphoreType.DMA((slabs,)),
            pltpu.SemaphoreType.DMA((3,)),
            pltpu.SemaphoreType.DMA((3,)),
        ],
        compiler_params=pltpu.CompilerParams(
            collective_id=0, has_side_effects=True, vmem_limit_bytes=24 << 20),
    )(*[pltpu.with_memory_space_constraint(value, pltpu.HBM) for value in (vector, gates)])
    return result.reshape(layout)


def tiled(order, count):
    return count > 1 and count & (count - 1) == 0 and order % (8 * count) == 0


def solution(mesh):
    wide, narrow = mesh.shape["wide"], mesh.shape["narrow"]

    def shards(amplitudes, gates):
        order = amplitudes.shape[4]
        if tiled(order, wide) and tiled(order, narrow) and wide * narrow <= 128:
            return fused(wide, narrow, amplitudes, gates)
        return plain(amplitudes, gates)

    return jax.shard_map(
        shards,
        mesh=mesh,
        in_specs=(P(None, None, "wide", "narrow", None, None), P()),
        out_specs=P(None, None, "wide", "narrow", None, None),
        check_vma=False,
    )
```

```python
import functools

import jax
import jax.numpy as jnp
from jax import lax
from jax.experimental import pallas as pl
from jax.experimental.pallas import tpu as pltpu
from jax.sharding import PartitionSpec as P

precise = lax.Precision.HIGHEST
MESH = pl.DeviceIdType.MESH
F32 = jnp.float32
BF16 = jnp.bfloat16
EARLY_AT = 5
DEFER = (0, 1)
DEFER_AT = 3
TAIL = 1


def blocks(matrix):
    return jnp.stack([jnp.stack([matrix[0], -matrix[1]]), jnp.stack([matrix[1], matrix[0]])])


def on_rows(vector, matrix):
    return jnp.einsum("cdjk,drkb->crjb", blocks(matrix), vector, precision=precise)


def on_columns(vector, matrix):
    return jnp.einsum("cdjk,drak->craj", blocks(matrix), vector, precision=precise)


def plain(amplitudes, gates):
    layout = amplitudes.shape
    slabs, order = layout[1], layout[4]
    vector = amplitudes.reshape(2, slabs, order, order)
    vector = on_columns(on_rows(vector, gates[0, 0]), gates[0, 1])
    vector = lax.all_to_all(vector.reshape(layout), "wide", split_axis=4, concat_axis=2, tiled=True)
    vector = vector.reshape(2, slabs, order, order)
    vector = on_columns(on_rows(vector, gates[1, 0]), gates[1, 1])
    vector = lax.all_to_all(vector.reshape(layout), "narrow", split_axis=4, concat_axis=3, tiled=True)
    vector = vector.reshape(2, slabs, order, order)
    vector = on_columns(on_rows(vector, gates[2, 0]), gates[2, 1])
    return vector.reshape(layout)


def partner(me, mask, count):
    out, bit = 0, 1
    while bit < count:
        digit = me // bit % 2
        if mask & bit:
            digit = 1 - digit
        out = out + digit * bit
        bit *= 2
    return out


def far_first(count):
    return sorted(range(1, count), key=lambda m: (-bin(m >> 1).count("1"), -m))


def split(value):
    high = value.astype(BF16)
    return high, (value - high.astype(F32)).astype(BF16)


def real_form(matrix):
    re, im = matrix[0], matrix[1]
    return jnp.concatenate(
        [jnp.concatenate([re, -im], axis=1), jnp.concatenate([im, re], axis=1)], axis=0
    )


def kernel(wide, narrow, early, amp, gates, out, x, g, y, yr, z, zr, left, right,
           met, load_sem, gate_sem, ws_sem, wr_sem, ns_sem, nr_sem, es_sem, er_sem):
    slabs, order = amp.shape[1], amp.shape[2]
    last = slabs - 1
    hw, hn = order // wide, order // narrow
    w, n = lax.axis_index("wide"), lax.axis_index("narrow")
    wide_masks = far_first(wide)
    narrow_masks = list(range(1, narrow))

    near = [i for i, mask in enumerate(wide_masks) if bin(mask >> 1).count("1") < 2]
    distant = [i for i in range(wide - 1) if i not in near]
    relayed = wide == 8
    greeted = near if relayed else list(range(wide - 1))

    barrier = pltpu.get_barrier_semaphore()
    for mask in [wide_masks[i] for i in greeted]:
        pl.semaphore_signal(barrier, inc=1, device_id=(partner(w, mask, wide), n), device_id_type=MESH)
    for mask in narrow_masks:
        pl.semaphore_signal(barrier, inc=1, device_id=(w, partner(n, mask, narrow)), device_id_type=MESH)

    def load(c):
        return pltpu.make_async_copy(amp.at[:, c], x.at[:, c], load_sem.at[c])

    def load_gate(t, k):
        return pltpu.make_async_copy(gates.at[t, k], g.at[t, k], gate_sem.at[t, k])

    load_gate(0, 0).start()
    if early:
        load(last).start()
    load(0).start()
    for t in range(3):
        for k in range(2):
            if (t, k) != (0, 0):
                load_gate(t, k).start()
    for c in range(1, last if early else slabs):
        load(c).start()

    def send_wide(c, i):
        there = partner(w, wide_masks[i], wide)
        return pltpu.make_async_remote_copy(
            src_ref=y.at[c, :, pl.ds(pl.multiple_of(there * hw, hw), hw), :],
            dst_ref=yr.at[c, :, pl.ds(pl.multiple_of(w * hw, hw), hw), :],
            send_sem=ws_sem.at[0], recv_sem=wr_sem.at[c],
            device_id=(there, n), device_id_type=MESH)

    def send_narrow(c, i):
        there = partner(n, narrow_masks[i], narrow)
        if narrow == 4:
            there = [partner(n, 1, narrow), 3 - 3 * (n // 2), 2 - n // 2][i]
        return pltpu.make_async_remote_copy(
            src_ref=z.at[c, :, pl.ds(pl.multiple_of(there * hn, hn), hn), :],
            dst_ref=zr.at[c, :, pl.ds(pl.multiple_of(n * hn, hn), hn), :],
            send_sem=ns_sem.at[0], recv_sem=nr_sem.at[c],
            device_id=(w, there), device_id_type=MESH)

    def send_early():
        return pltpu.make_async_remote_copy(
            src_ref=x.at[:, last], dst_ref=x.at[:, slabs],
            send_sem=es_sem.at[0], recv_sem=er_sem.at[0],
            device_id=(w, partner(n, 3, narrow)), device_id_type=MESH)

    def send_half(k):
        there = partner(n, 1, narrow)
        index = partner(n, 3 * k, narrow)
        return pltpu.make_async_remote_copy(
            src_ref=z.at[last + k, :, pl.ds(pl.multiple_of(there * hn, hn), hn), :],
            dst_ref=zr.at[last, :, pl.ds(pl.multiple_of(index * hn, hn), hn), :],
            send_sem=es_sem.at[1 + k], recv_sem=er_sem.at[1 + k],
            device_id=(w, there), device_id_type=MESH)

    def arrived(ref, sem):
        pltpu.make_async_copy(ref, ref, sem).wait()

    def prepare(t):
        load_gate(t, 0).wait()
        high, low = split(real_form(g[t, 0]))
        left[t] = jnp.concatenate([high, low, high], axis=1)

    def rows(t, value):
        high, low = split(value.reshape(2 * order, order))
        stacked = jnp.concatenate([high, high, low], axis=0)
        return jnp.dot(left[t], stacked, preferred_element_type=F32)

    def columns(value):
        high, low = split(jnp.concatenate([value[:order], value[order:]], axis=1))
        stacked = jnp.concatenate([high, low, high], axis=1)
        return jnp.dot(stacked, right[...], preferred_element_type=F32)

    def first(c, loaded=False):
        if not loaded:
            load(c).wait()
        y[c] = rows(0, x[:, c]).reshape(2, order, order)

    def start_wide(c, some=None):
        for i in range(wide - 1) if some is None else some:
            send_wide(c, i).start()

    def meet():
        pl.semaphore_wait(barrier, len(greeted) + narrow - 1)
        if relayed:
            pl.semaphore_signal(met, inc=1, device_id=(partner(w, 2, wide), n), device_id_type=MESH)

    def meet_distant():
        if relayed:
            pl.semaphore_wait(met, 1)

    prepare(0)
    first(0)
    if early:
        load(last).wait()
    meet()
    if early:
        send_early().start()
    start_wide(0, near)
    first(1)
    meet_distant()
    start_wide(0, distant)
    start_wide(1)

    @pl.loop(2, last if early else slabs)
    def _(c):
        first(c)
        start_wide(c)

    if early:
        first(last, True)
        start_wide(last)

    def second(c, with_columns, with_narrow=None):
        own = pl.ds(pl.multiple_of(w * hw, hw), hw)
        yr[c, :, own, :] = y[c, :, own, :]
        arrived(yr.at[c, :, pl.ds(0, hw * (wide - 1)), :], wr_sem.at[c])
        value = rows(1, yr[c])
        if with_columns:
            value = columns(value)
            z[c, 0] = value[:, :order]
            z[c, 1] = value[:, order:]
        else:
            z[c] = value.reshape(2, order, order)
        for i in range(narrow - 1) if with_narrow is None else with_narrow:
            send_narrow(c, i).start()

    prepare(1)
    for t in range(3):
        load_gate(t, 1).wait()
    product = g[0, 1].reshape(2 * order, order)
    for t in (1, 2):
        product = jnp.dot(real_form(g[t, 1]), product, precision=precise, preferred_element_type=F32)
    re, im = product[:order].T, product[order:].T
    high, low = split(jnp.concatenate(
        [jnp.concatenate([re, im], axis=1), jnp.concatenate([-im, re], axis=1)], axis=0))
    right[...] = jnp.concatenate([high, high, low], axis=0)
    prepare(2)

    second(0, False)

    if early:
        @pl.loop(1, DEFER_AT)
        def _(c):
            second(c, True)

        @pl.loop(DEFER_AT, EARLY_AT)
        def _(c):
            second(c, True, DEFER)

        send_early().wait_recv()
        first(slabs, True)
        start_wide(slabs)

        @pl.loop(EARLY_AT, last - TAIL)
        def _(c):
            second(c, True, DEFER)

        @pl.loop(last, slabs + 1)
        def _(c):
            second(c, False, [])

        for k in range(2):
            send_half(k).start()
            index = partner(n, 3 * k, narrow)
            rows_to = pl.ds(pl.multiple_of(index * hn, hn), hn)
            rows_from = pl.ds(pl.multiple_of(n * hn, hn), hn)
            zr[last, :, rows_to, :] = z[last + k, :, rows_from, :]

        @pl.loop(last - TAIL, last)
        def _(c):
            second(c, True, DEFER)

        @pl.loop(DEFER_AT, last)
        def _(c):
            for i in range(narrow - 1):
                if i not in DEFER:
                    send_narrow(c, i).start()
    else:
        @pl.loop(1, slabs)
        def _(c):
            second(c, True)

    def third(c, with_columns, exchanged=False):
        if not exchanged:
            own = pl.ds(pl.multiple_of(n * hn, hn), hn)
            zr[c, :, own, :] = z[c, :, own, :]
            arrived(zr.at[c, :, pl.ds(0, hn * (narrow - 1)), :], nr_sem.at[c])
        value = rows(2, zr[c])
        if with_columns:
            value = columns(value)
            out[0, c] = value[:, :order]
            out[1, c] = value[:, order:]
        else:
            out[0, c] = value[:order]
            out[1, c] = value[order:]

    third(0, True)
    if early:
        @pl.loop(1, last - TAIL)
        def _(c):
            third(c, False)

        for k in range(2):
            send_half(k).wait_recv()
        third(last, True, True)

        @pl.loop(last - TAIL, last)
        def _(c):
            third(c, False)
    else:
        @pl.loop(1, slabs)
        def _(c):
            third(c, False)

    arrived(y.at[:, :, pl.ds(0, hw * (wide - 1)), :], ws_sem.at[0])
    sent = z.at[pl.ds(0, last if early else slabs), :, pl.ds(0, hn * (narrow - 1)), :]
    arrived(sent, ns_sem.at[0])

    if early:
        send_early().wait_send()
        for k in range(2):
            send_half(k).wait_send()


def fused(wide, narrow, amplitudes, gates):
    layout = amplitudes.shape
    slabs, order = layout[1], layout[4]
    vector = amplitudes.reshape(2, slabs, order, order)
    early = narrow == 4 and slabs > EARLY_AT + TAIL
    slots = slabs + early
    slab_buffer = pltpu.VMEM((slots, 2, order, order), F32)
    result = pl.pallas_call(
        functools.partial(kernel, wide, narrow, early),
        out_shape=jax.ShapeDtypeStruct(vector.shape, F32),
        in_specs=[pl.BlockSpec(memory_space=pl.ANY)] * 2,
        out_specs=pl.BlockSpec(memory_space=pltpu.VMEM),
        scratch_shapes=[
            pltpu.VMEM((2, slots, order, order), F32),
            pltpu.VMEM(gates.shape, F32),
            slab_buffer, slab_buffer, slab_buffer, slab_buffer,
            pltpu.VMEM((3, 2 * order, 6 * order), BF16),
            pltpu.VMEM((6 * order, 2 * order), BF16),
            pltpu.SemaphoreType.REGULAR,
            pltpu.SemaphoreType.DMA((slabs,)),
            pltpu.SemaphoreType.DMA((3, 2)),
            pltpu.SemaphoreType.DMA((1,)),
            pltpu.SemaphoreType.DMA((slots,)),
            pltpu.SemaphoreType.DMA((1,)),
            pltpu.SemaphoreType.DMA((slabs,)),
            pltpu.SemaphoreType.DMA((3,)),
            pltpu.SemaphoreType.DMA((3,)),
        ],
        compiler_params=pltpu.CompilerParams(
            collective_id=0, has_side_effects=True, vmem_limit_bytes=24 << 20),
    )(*[pltpu.with_memory_space_constraint(value, pltpu.HBM) for value in (vector, gates)])
    return result.reshape(layout)


def tiled(order, count):
    return count > 1 and count & (count - 1) == 0 and order % (8 * count) == 0


def solution(mesh):
    wide, narrow = mesh.shape["wide"], mesh.shape["narrow"]

    def shards(amplitudes, gates):
        order = amplitudes.shape[4]
        if tiled(order, wide) and tiled(order, narrow) and wide * narrow <= 128:
            return fused(wide, narrow, amplitudes, gates)
        return plain(amplitudes, gates)

    return jax.shard_map(
        shards,
        mesh=mesh,
        in_specs=(P(None, None, "wide", "narrow", None, None), P()),
        out_specs=P(None, None, "wide", "narrow", None, None),
        check_vma=False,
    )
```

```python
import functools

import jax
import jax.numpy as jnp
from jax import lax
from jax.experimental import pallas as pl
from jax.experimental.pallas import tpu as pltpu
from jax.sharding import PartitionSpec as P

precise = lax.Precision.HIGHEST
MESH = pl.DeviceIdType.MESH
F32 = jnp.float32
BF16 = jnp.bfloat16
EARLY_AT = 5
DEFER_AT = 3


def blocks(matrix):
    return jnp.stack([jnp.stack([matrix[0], -matrix[1]]), jnp.stack([matrix[1], matrix[0]])])


def on_rows(vector, matrix):
    return jnp.einsum("cdjk,drkb->crjb", blocks(matrix), vector, precision=precise)


def on_columns(vector, matrix):
    return jnp.einsum("cdjk,drak->craj", blocks(matrix), vector, precision=precise)


def plain(amplitudes, gates):
    layout = amplitudes.shape
    slabs, order = layout[1], layout[4]
    vector = amplitudes.reshape(2, slabs, order, order)
    vector = on_columns(on_rows(vector, gates[0, 0]), gates[0, 1])
    vector = lax.all_to_all(vector.reshape(layout), "wide", split_axis=4, concat_axis=2, tiled=True)
    vector = vector.reshape(2, slabs, order, order)
    vector = on_columns(on_rows(vector, gates[1, 0]), gates[1, 1])
    vector = lax.all_to_all(vector.reshape(layout), "narrow", split_axis=4, concat_axis=3, tiled=True)
    vector = vector.reshape(2, slabs, order, order)
    vector = on_columns(on_rows(vector, gates[2, 0]), gates[2, 1])
    return vector.reshape(layout)


def partner(me, mask, count):
    out, bit = 0, 1
    while bit < count:
        digit = me // bit % 2
        if mask & bit:
            digit = 1 - digit
        out = out + digit * bit
        bit *= 2
    return out


def far_first(count):
    return sorted(range(1, count), key=lambda m: (-bin(m >> 1).count("1"), -m))


def turn(w, count):
    if count != 8:
        return w
    chip = w // 2
    return 2 * (chip % 2 + chip // 2) + 1 - w % 2


def greeters(w, count):
    if count != 8:
        return w
    level = turn(w, count) // 2
    return level * (level + 1) + 1 - w % 2


def split(value):
    high = value.astype(BF16)
    return high, (value - high.astype(F32)).astype(BF16)


def real_form(matrix):
    re, im = matrix[0], matrix[1]
    return jnp.concatenate(
        [jnp.concatenate([re, -im], axis=1), jnp.concatenate([im, re], axis=1)], axis=0
    )


def kernel(wide, narrow, early, amp, gates, out, zr, left, x, g, y, yr, z, right,
           met, x_sem, g_sem, ws_sem, wr_sem, ns_sem, nr_sem, es_sem, er_sem):
    slabs, order = amp.shape[1], amp.shape[2]
    last = slabs - 1
    hw, hn = order // wide, order // narrow
    w, n = lax.axis_index("wide"), lax.axis_index("narrow")
    wide_masks = far_first(wide)
    narrow_masks = list(range(1, narrow))

    def wait(ref, sem):
        pltpu.make_async_copy(ref, ref, sem).wait()

    def load(i):
        part = pl.ds(i, 1) if i < 2 else pl.ds(2, slabs - 2)
        return pltpu.make_async_copy(amp.at[:, part], x.at[:, part], x_sem.at[i])

    def load_gate(i):
        part = pl.ds(0, 1) if i == 0 else pl.ds(1, 5)
        return pltpu.make_async_copy(gates.at[part], g.at[part], g_sem.at[i])

    def apart(mask):
        if wide != 8 or mask < 6:
            return False
        return turn(w, wide) // 2 == 1

    def comes_first(there, mask):
        return (turn(there, wide) < turn(w, wide)) & jnp.logical_not(apart(mask))

    def follows(there, mask):
        return (turn(there, wide) > turn(w, wide)) & jnp.logical_not(apart(mask))

    def greet(after):
        for mask in wide_masks:
            there = partner(w, mask, wide)

            @pl.when(comes_first(there, mask) if not after else follows(there, mask))
            def _():
                sem = pltpu.get_barrier_semaphore() if after else met.at[mask - 1]
                pl.semaphore_signal(sem, inc=1, device_id=(there, n), device_id_type=MESH)
        for mask in narrow_masks:
            there = partner(n, mask, narrow)

            @pl.when((there > n) == after)
            def _():
                sem = pltpu.get_barrier_semaphore() if after else met.at[wide + mask - 2]
                pl.semaphore_signal(sem, inc=1, device_id=(w, there), device_id_type=MESH)

    def send_wide(c, i):
        there = partner(w, wide_masks[i], wide)
        return pltpu.make_async_remote_copy(
            src_ref=y.at[c, :, pl.ds(pl.multiple_of(there * hw, hw), hw), :],
            dst_ref=yr.at[c, :, pl.ds(pl.multiple_of(w * hw, hw), hw), :],
            send_sem=ws_sem.at[0], recv_sem=wr_sem.at[c],
            device_id=(there, n), device_id_type=MESH)

    def send_narrow(c, i):
        there = partner(n, narrow_masks[i], narrow)
        if narrow == 4:
            there = [partner(n, 1, narrow), 3 - 3 * (n // 2), 2 - n // 2][i]
        return pltpu.make_async_remote_copy(
            src_ref=z.at[c, :, pl.ds(pl.multiple_of(there * hn, hn), hn), :],
            dst_ref=zr.at[c, :, pl.ds(pl.multiple_of(n * hn, hn), hn), :],
            send_sem=ns_sem.at[0], recv_sem=nr_sem.at[c],
            device_id=(w, there), device_id_type=MESH)

    def send_early():
        return pltpu.make_async_remote_copy(
            src_ref=amp.at[:, last], dst_ref=x.at[:, slabs],
            send_sem=es_sem.at[0], recv_sem=er_sem.at[0],
            device_id=(w, partner(n, 3, narrow)), device_id_type=MESH)

    def send_half(k):
        there = partner(n, 1, narrow)
        index = partner(n, 3 * k, narrow)
        return pltpu.make_async_remote_copy(
            src_ref=z.at[last + k, :, pl.ds(pl.multiple_of(there * hn, hn), hn), :],
            dst_ref=zr.at[last, :, pl.ds(pl.multiple_of(index * hn, hn), hn), :],
            send_sem=es_sem.at[1], recv_sem=er_sem.at[1],
            device_id=(w, there), device_id_type=MESH)

    def prepare(t):
        high, low = split(real_form(g[2 * t]))
        left[t] = jnp.concatenate([high, low, high], axis=1)

    def rows(t, value):
        high, low = split(value.reshape(2 * order, order))
        stacked = jnp.concatenate([high, high, low], axis=0)
        return jnp.dot(left[t], stacked, preferred_element_type=F32)

    def columns(value):
        high, low = split(jnp.concatenate([value[:order], value[order:]], axis=1))
        stacked = jnp.concatenate([high, low, high], axis=1)
        return jnp.dot(stacked, right[...], preferred_element_type=F32)

    def first(c):
        y[c] = rows(0, x[:, c]).reshape(2, order, order)

    def start_wide_known(c, known):
        for mask in wide_masks if known else wide_masks[::-1]:
            there = partner(w, mask, wide)

            @pl.when(comes_first(there, mask) == known)
            def _():
                if not known:
                    @pl.when(follows(there, mask))
                    def _():
                        pl.semaphore_wait(met.at[mask - 1], 1)
                send_wide(c, wide_masks.index(mask)).start()

    def start_wide(c):
        for i in range(wide - 1):
            send_wide(c, i).start()

    def second(c, with_columns, to):
        own = pl.ds(pl.multiple_of(w * hw, hw), hw)
        yr[c, :, own, :] = y[c, :, own, :]
        wait(yr.at[c, :, pl.ds(0, hw * (wide - 1)), :], wr_sem.at[c])
        value = rows(1, yr[c])
        if with_columns:
            value = columns(value)
            z[c, 0] = value[:, :order]
            z[c, 1] = value[:, order:]
        else:
            z[c] = value.reshape(2, order, order)
        for i in to:
            send_narrow(c, i).start()

    def exchanged(c):
        own = pl.ds(pl.multiple_of(n * hn, hn), hn)
        zr[c, :, own, :] = z[c, :, own, :]
        wait(zr.at[c, :, pl.ds(0, hn * (narrow - 1)), :], nr_sem.at[c])

    def third(c, with_columns, whole=False):
        if not whole:
            exchanged(c)
        value = rows(2, zr[c])
        if with_columns:
            value = columns(value)
            out[0, c] = value[:, :order]
            out[1, c] = value[:, order:]
        else:
            out[0, c] = value[:order]
            out[1, c] = value[order:]

    load_gate(0).start()
    load(0).start()
    greet(True)
    load(1).start()
    load_gate(1).start()
    load(2).start()
    expected = greeters(w, wide) + n

    @pl.when(expected > 0)
    def _():
        pl.semaphore_wait(pltpu.get_barrier_semaphore(), expected)
    if early:
        @pl.when(n >= 2)
        def _():
            send_early().start()
    greet(False)

    load_gate(0).wait()
    prepare(0)
    load(0).wait()
    first(0)
    start_wide_known(0, True)
    if early:
        @pl.when(n == 1)
        def _():
            pl.semaphore_wait(met.at[wide + 1], 1)
            send_early().start()
    start_wide_known(0, False)
    load(1).wait()
    first(1)
    start_wide(1)
    if early:
        @pl.when(n == 0)
        def _():
            pl.semaphore_wait(met.at[wide + 1], 1)
            send_early().start()
    load(2).wait()

    @pl.loop(2, slabs)
    def _(c):
        first(c)
        start_wide(c)

    load_gate(1).wait()
    product = g[1].reshape(2 * order, order)
    for t in (1, 2):
        product = jnp.dot(real_form(g[2 * t + 1]), product, precision=precise, preferred_element_type=F32)
    re, im = product[:order].T, product[order:].T
    high, low = split(jnp.concatenate(
        [jnp.concatenate([re, im], axis=1), jnp.concatenate([-im, re], axis=1)], axis=0))
    right[...] = jnp.concatenate([high, high, low], axis=0)
    prepare(1)
    prepare(2)
    for mask in narrow_masks:
        if not (early and mask == 3):
            @pl.when(partner(n, mask, narrow) > n)
            def _():
                pl.semaphore_wait(met.at[wide + mask - 2], 1)

    everywhere = list(range(narrow - 1))
    if early:
        soon, later = everywhere[:-1], everywhere[-1:]
        second(0, False, everywhere)

        @pl.loop(1, DEFER_AT)
        def _(c):
            second(c, True, everywhere)

        @pl.loop(DEFER_AT, EARLY_AT)
        def _(c):
            second(c, True, soon)

        send_early().wait_recv()
        first(slabs)
        start_wide(slabs)

        @pl.loop(EARLY_AT, last - 1)
        def _(c):
            second(c, True, soon)

        @pl.loop(last, slabs + 1)
        def _(c):
            second(c, False, [])

        for k in range(2):
            send_half(k).start()
            index = partner(n, 3 * k, narrow)
            rows_to = pl.ds(pl.multiple_of(index * hn, hn), hn)
            rows_from = pl.ds(pl.multiple_of(n * hn, hn), hn)
            zr[last, :, rows_to, :] = z[last + k, :, rows_from, :]

        second(last - 1, True, soon)

        @pl.loop(DEFER_AT, last)
        def _(c):
            for i in later:
                send_narrow(c, i).start()
    else:
        second(0, False, everywhere)

        @pl.loop(1, slabs)
        def _(c):
            second(c, True, everywhere)

    third(0, True)
    if early:
        @pl.loop(1, last - 1)
        def _(c):
            third(c, False)

        wait(zr.at[last, :, pl.ds(0, 2 * hn), :], er_sem.at[1])
        third(last, True, True)
        exchanged(last - 1)
    else:
        @pl.loop(1, last)
        def _(c):
            third(c, False)

        exchanged(last)

    wait(y.at[:, :, pl.ds(0, hw * (wide - 1)), :], ws_sem.at[0])
    wait(z.at[pl.ds(0, last if early else slabs), :, pl.ds(0, hn * (narrow - 1)), :], ns_sem.at[0])
    if early:
        send_early().wait_send()
        wait(z.at[last, :, pl.ds(0, 2 * hn), :], es_sem.at[1])


def finish(c, done, arrived, left, out, value, sem):
    slabs, order = done.shape[1], done.shape[2]
    others = [i for i in range(slabs) if i != c]

    def write(i):
        return pltpu.make_async_copy(done.at[:, i], out.at[:, i], sem.at[0])

    for i in others:
        write(i).start()
    high, low = split(arrived[c].reshape(2 * order, order))
    stacked = jnp.concatenate([high, high, low], axis=0)
    value[...] = jnp.dot(left[2], stacked, preferred_element_type=F32).reshape(2, order, order)
    write_last = pltpu.make_async_copy(value, out.at[:, c], sem.at[1])
    write_last.start()
    for i in others:
        write(i).wait()
    write_last.wait()


def fused(wide, narrow, amplitudes, gates):
    layout = amplitudes.shape
    slabs, order = layout[1], layout[4]
    vector = amplitudes.reshape(2, slabs, order, order)
    matrices = gates.reshape(6, 2, order, order)
    early = narrow == 4 and slabs == 8
    slots = slabs + early
    slab_buffer = pltpu.VMEM((slots, 2, order, order), F32)
    done, arrived, left = pl.pallas_call(
        functools.partial(kernel, wide, narrow, early),
        out_shape=[
            jax.ShapeDtypeStruct(vector.shape, F32),
            jax.ShapeDtypeStruct((slabs, 2, order, order), F32),
            jax.ShapeDtypeStruct((3, 2 * order, 6 * order), BF16),
        ],
        in_specs=[pl.BlockSpec(memory_space=pl.ANY)] * 2,
        out_specs=[pl.BlockSpec(memory_space=pltpu.VMEM)] * 3,
        scratch_shapes=[
            pltpu.VMEM((2, slots, order, order), F32),
            pltpu.VMEM(matrices.shape, F32),
            slab_buffer, slab_buffer, slab_buffer,
            pltpu.VMEM((6 * order, 2 * order), BF16),
            pltpu.SemaphoreType.REGULAR((wide + narrow - 2,)),
            pltpu.SemaphoreType.DMA((3,)),
            pltpu.SemaphoreType.DMA((2,)),
            pltpu.SemaphoreType.DMA((1,)),
            pltpu.SemaphoreType.DMA((slots,)),
            pltpu.SemaphoreType.DMA((1,)),
            pltpu.SemaphoreType.DMA((slabs - early,)),
            pltpu.SemaphoreType.DMA((2,)),
            pltpu.SemaphoreType.DMA((2,)),
        ],
        compiler_params=pltpu.CompilerParams(
            collective_id=0, has_side_effects=True, vmem_limit_bytes=24 << 20),
    )(*[pltpu.with_memory_space_constraint(value, pltpu.HBM) for value in (vector, matrices)])
    result = pl.pallas_call(
        functools.partial(finish, slabs - 1 - early),
        out_shape=jax.ShapeDtypeStruct(vector.shape, F32),
        in_specs=[pl.BlockSpec(memory_space=pltpu.VMEM)] * 3,
        out_specs=pl.BlockSpec(memory_space=pltpu.HBM),
        scratch_shapes=[
            pltpu.VMEM((2, order, order), F32),
            pltpu.SemaphoreType.DMA((2,)),
        ],
        compiler_params=pltpu.CompilerParams(vmem_limit_bytes=8 << 20),
    )(done, arrived, left)
    return result.reshape(layout)


def tiled(order, count):
    return count > 1 and count & (count - 1) == 0 and order % (8 * count) == 0


def solution(mesh):
    wide, narrow = mesh.shape["wide"], mesh.shape["narrow"]

    def shards(amplitudes, gates):
        order, slabs = amplitudes.shape[4], amplitudes.shape[1]
        if tiled(order, wide) and tiled(order, narrow) and wide * narrow <= 128 and slabs > 2:
            return fused(wide, narrow, amplitudes, gates)
        return plain(amplitudes, gates)

    return jax.shard_map(
        shards,
        mesh=mesh,
        in_specs=(P(None, None, "wide", "narrow", None, None), P()),
        out_specs=P(None, None, "wide", "narrow", None, None),
        check_vma=False,
    )
```

```python
import functools

import jax
import jax.numpy as jnp
from jax import lax
from jax.experimental import pallas as pl
from jax.experimental.pallas import tpu as pltpu
from jax.sharding import PartitionSpec as P

precise = lax.Precision.HIGHEST
MESH = pl.DeviceIdType.MESH
F32 = jnp.float32
BF16 = jnp.bfloat16
EARLY_AT = 5
DEFER_AT = 3
AHEAD = 4


def blocks(matrix):
    return jnp.stack([jnp.stack([matrix[0], -matrix[1]]), jnp.stack([matrix[1], matrix[0]])])


def on_rows(vector, matrix):
    return jnp.einsum("cdjk,drkb->crjb", blocks(matrix), vector, precision=precise)


def on_columns(vector, matrix):
    return jnp.einsum("cdjk,drak->craj", blocks(matrix), vector, precision=precise)


def plain(amplitudes, gates):
    layout = amplitudes.shape
    slabs, order = layout[1], layout[4]
    vector = amplitudes.reshape(2, slabs, order, order)
    vector = on_columns(on_rows(vector, gates[0, 0]), gates[0, 1])
    vector = lax.all_to_all(vector.reshape(layout), "wide", split_axis=4, concat_axis=2, tiled=True)
    vector = vector.reshape(2, slabs, order, order)
    vector = on_columns(on_rows(vector, gates[1, 0]), gates[1, 1])
    vector = lax.all_to_all(vector.reshape(layout), "narrow", split_axis=4, concat_axis=3, tiled=True)
    vector = vector.reshape(2, slabs, order, order)
    vector = on_columns(on_rows(vector, gates[2, 0]), gates[2, 1])
    return vector.reshape(layout)


def partner(me, mask, count):
    out, bit = 0, 1
    while bit < count:
        digit = me // bit % 2
        if mask & bit:
            digit = 1 - digit
        out = out + digit * bit
        bit *= 2
    return out


def far_first(count):
    return sorted(range(1, count), key=lambda m: (-bin(m >> 1).count("1"), -m))


def turn(w, count):
    if count != 8:
        return w
    chip = w // 2
    return 2 * (chip % 2 + chip // 2) + 1 - w % 2


def greeters(w, count):
    if count != 8:
        return w
    level = turn(w, count) // 2
    return level * (level + 1) + 1 - w % 2


def split(value):
    high = value.astype(BF16)
    return high, (value - high.astype(F32)).astype(BF16)


def real_form(matrix):
    re, im = matrix[0], matrix[1]
    return jnp.concatenate(
        [jnp.concatenate([re, -im], axis=1), jnp.concatenate([im, re], axis=1)], axis=0
    )


def kernel(wide, narrow, early, amp, gates, out, zr, left, x, g, y, yr, z, right,
           met, x_sem, g_sem, ws_sem, wr_sem, ns_sem, nr_sem, es_sem, er_sem):
    slabs, order = amp.shape[1], amp.shape[2]
    last = slabs - 1
    hw, hn = order // wide, order // narrow
    w, n = lax.axis_index("wide"), lax.axis_index("narrow")
    wide_masks = far_first(wide)
    narrow_masks = list(range(1, narrow))

    def wait(ref, sem):
        pltpu.make_async_copy(ref, ref, sem).wait()

    def load(i):
        part = pl.ds(i, 1) if i < 2 else pl.ds(2, slabs - 2)
        return pltpu.make_async_copy(amp.at[:, part], x.at[:, part], x_sem.at[i])

    def load_gate(i):
        part = pl.ds(0, 1) if i == 0 else pl.ds(1, 5)
        return pltpu.make_async_copy(gates.at[part], g.at[part], g_sem.at[i])

    def apart(mask):
        if wide != 8 or mask < 6:
            return False
        return turn(w, wide) // 2 == 1

    def comes_first(there, mask):
        return (turn(there, wide) < turn(w, wide)) & jnp.logical_not(apart(mask))

    def follows(there, mask):
        return (turn(there, wide) > turn(w, wide)) & jnp.logical_not(apart(mask))

    def hurried(here, there):
        return (here == 2) & (there == 1) if early else False

    def greet(after):
        for mask in wide_masks:
            there = partner(w, mask, wide)

            @pl.when(comes_first(there, mask) if not after else follows(there, mask))
            def _():
                sem = pltpu.get_barrier_semaphore() if after else met.at[mask - 1]
                pl.semaphore_signal(sem, inc=1, device_id=(there, n), device_id_type=MESH)
        for mask in narrow_masks:
            there = partner(n, mask, narrow)

            @pl.when((there > n) | hurried(n, there) if after else (there < n) & jnp.logical_not(hurried(n, there)))
            def _():
                sem = pltpu.get_barrier_semaphore() if after else met.at[wide + mask - 2]
                pl.semaphore_signal(sem, inc=1, device_id=(w, there), device_id_type=MESH)

    def send_wide(c, i):
        there = partner(w, wide_masks[i], wide)
        return pltpu.make_async_remote_copy(
            src_ref=y.at[c, :, pl.ds(pl.multiple_of(there * hw, hw), hw), :],
            dst_ref=yr.at[c, :, pl.ds(pl.multiple_of(w * hw, hw), hw), :],
            send_sem=ws_sem.at[0], recv_sem=wr_sem.at[c],
            device_id=(there, n), device_id_type=MESH)

    def send_narrow(c, i):
        there = partner(n, narrow_masks[i], narrow)
        if narrow == 4:
            there = [partner(n, 1, narrow), 3 - 3 * (n // 2), 2 - n // 2][i]
        return pltpu.make_async_remote_copy(
            src_ref=z.at[c, :, pl.ds(pl.multiple_of(there * hn, hn), hn), :],
            dst_ref=zr.at[c, :, pl.ds(pl.multiple_of(n * hn, hn), hn), :],
            send_sem=ns_sem.at[0], recv_sem=nr_sem.at[c],
            device_id=(w, there), device_id_type=MESH)

    def send_early():
        return pltpu.make_async_remote_copy(
            src_ref=amp.at[:, last], dst_ref=x.at[:, slabs],
            send_sem=es_sem.at[0], recv_sem=er_sem.at[0],
            device_id=(w, partner(n, 3, narrow)), device_id_type=MESH)

    def send_half(k):
        there = partner(n, 1, narrow)
        index = partner(n, 3 * k, narrow)
        return pltpu.make_async_remote_copy(
            src_ref=z.at[last + k, :, pl.ds(pl.multiple_of(there * hn, hn), hn), :],
            dst_ref=zr.at[last, :, pl.ds(pl.multiple_of(index * hn, hn), hn), :],
            send_sem=es_sem.at[1], recv_sem=er_sem.at[1],
            device_id=(w, there), device_id_type=MESH)

    def prepare(t):
        high, low = split(real_form(g[2 * t]))
        left[t] = jnp.concatenate([high, low, high], axis=1)

    def rows(t, value):
        high, low = split(value.reshape(2 * order, order))
        stacked = jnp.concatenate([high, high, low], axis=0)
        return jnp.dot(left[t], stacked, preferred_element_type=F32)

    def columns(value):
        high, low = split(jnp.concatenate([value[:order], value[order:]], axis=1))
        stacked = jnp.concatenate([high, low, high], axis=1)
        return jnp.dot(stacked, right[...], preferred_element_type=F32)

    def first(c):
        y[c] = rows(0, x[:, c]).reshape(2, order, order)

    def answered(mask):
        @pl.when(follows(partner(w, mask, wide), mask))
        def _():
            pl.semaphore_wait(met.at[mask - 1], 1)

    def start_wide_known(c, known):
        if not known and wide == 8:
            @pl.when(apart(6))
            def _():
                for mask in wide_masks[::-1]:
                    answered(mask)
                for mask in (7, 6):
                    send_wide(c, wide_masks.index(mask)).start()
        for mask in wide_masks if known else wide_masks[::-1]:
            there = partner(w, mask, wide)

            @pl.when(comes_first(there, mask) if known else follows(there, mask))
            def _():
                if not known:
                    @pl.when(jnp.logical_not(apart(6)))
                    def _():
                        answered(mask)
                send_wide(c, wide_masks.index(mask)).start()

    def start_wide(c):
        for i in range(wide - 1):
            send_wide(c, i).start()

    def second(c, with_columns, to):
        own = pl.ds(pl.multiple_of(w * hw, hw), hw)
        yr[c, :, own, :] = y[c, :, own, :]
        wait(yr.at[c, :, pl.ds(0, hw * (wide - 1)), :], wr_sem.at[c])
        value = rows(1, yr[c])
        if with_columns:
            value = columns(value)
            z[c, 0] = value[:, :order]
            z[c, 1] = value[:, order:]
        else:
            z[c] = value.reshape(2, order, order)
        for i in to:
            send_narrow(c, i).start()

    def start_ahead(c):
        if isinstance(c, int):
            if c + AHEAD < slabs:
                first(c + AHEAD)
                start_wide(c + AHEAD)
        else:
            @pl.when(c + AHEAD < slabs)
            def _():
                first(c + AHEAD)
                start_wide(c + AHEAD)

    def exchanged(c):
        own = pl.ds(pl.multiple_of(n * hn, hn), hn)
        zr[c, :, own, :] = z[c, :, own, :]
        wait(zr.at[c, :, pl.ds(0, hn * (narrow - 1)), :], nr_sem.at[c])

    def third(c, with_columns, whole=False):
        if not whole:
            exchanged(c)
        value = rows(2, zr[c])
        if with_columns:
            value = columns(value)
            out[0, c] = value[:, :order]
            out[1, c] = value[:, order:]
        else:
            out[0, c] = value[:order]
            out[1, c] = value[order:]

    load_gate(0).start()
    load(0).start()
    greet(True)
    load(1).start()
    load_gate(1).start()
    load(2).start()
    def meet():
        expected = greeters(w, wide) + n + jnp.where(n == 1, 1, 0) if early else greeters(w, wide) + n
        @pl.when(expected > 0)
        def _():
            pl.semaphore_wait(pltpu.get_barrier_semaphore(), expected)
        if early:
            @pl.when(n > 0)
            def _():
                send_early().start()
        greet(False)

    pl.when(n != 1)(meet) if early else meet()
    load_gate(0).wait()
    prepare(0)
    load(0).wait()
    first(0)
    if early:
        pl.when(n == 1)(meet)
    start_wide_known(0, True)
    load(1).wait()
    first(1)
    start_wide_known(0, False)
    start_wide(1)
    if early:
        @pl.when(n == 0)
        def _():
            pl.semaphore_wait(met.at[wide + 1], 1)
            send_early().start()
    load(2).wait()

    @pl.loop(2, AHEAD)
    def _(c):
        first(c)
        start_wide(c)

    load_gate(1).wait()
    product = g[1].reshape(2 * order, order)
    for t in (1, 2):
        product = jnp.dot(real_form(g[2 * t + 1]), product, precision=precise, preferred_element_type=F32)
    re, im = product[:order].T, product[order:].T
    high, low = split(jnp.concatenate(
        [jnp.concatenate([re, im], axis=1), jnp.concatenate([-im, re], axis=1)], axis=0))
    right[...] = jnp.concatenate([high, high, low], axis=0)
    prepare(1)
    prepare(2)

    for mask in narrow_masks:
        if not (early and mask == 3):
            @pl.when(partner(n, mask, narrow) > n)
            def _():
                pl.semaphore_wait(met.at[wide + mask - 2], 1)

    everywhere = list(range(narrow - 1))
    if early:
        soon, later = everywhere[:-1], everywhere[-1:]
        second(0, False, everywhere)
        start_ahead(0)

        @pl.loop(1, DEFER_AT)
        def _(c):
            second(c, True, everywhere)
            start_ahead(c)

        @pl.loop(DEFER_AT, EARLY_AT)
        def _(c):
            second(c, True, soon)
            start_ahead(c)

        send_early().wait_recv()
        first(slabs)
        start_wide(slabs)

        @pl.loop(EARLY_AT, last - 1)
        def _(c):
            second(c, True, soon)

        @pl.loop(last, slabs + 1)
        def _(c):
            second(c, False, [])

        for k in range(2):
            send_half(k).start()
            index = partner(n, 3 * k, narrow)
            rows_to = pl.ds(pl.multiple_of(index * hn, hn), hn)
            rows_from = pl.ds(pl.multiple_of(n * hn, hn), hn)
            zr[last, :, rows_to, :] = z[last + k, :, rows_from, :]

        second(last - 1, True, soon)

        @pl.loop(DEFER_AT, last)
        def _(c):
            for i in later:
                send_narrow(c, i).start()
    else:
        second(0, False, everywhere)
        start_ahead(0)

        @pl.loop(1, slabs)
        def _(c):
            second(c, True, everywhere)
            start_ahead(c)

    third(0, True)
    if early:
        @pl.loop(1, last - 1)
        def _(c):
            third(c, False)

        wait(zr.at[last, :, pl.ds(0, 2 * hn), :], er_sem.at[1])
        third(last, True, True)
        exchanged(last - 1)
    else:
        @pl.loop(1, last)
        def _(c):
            third(c, False)

        exchanged(last)

    wait(y.at[:, :, pl.ds(0, hw * (wide - 1)), :], ws_sem.at[0])
    wait(z.at[pl.ds(0, last if early else slabs), :, pl.ds(0, hn * (narrow - 1)), :], ns_sem.at[0])
    if early:
        send_early().wait_send()
        wait(z.at[last, :, pl.ds(0, 2 * hn), :], es_sem.at[1])


def finish(c, done, arrived, left, out, value, sem):
    slabs, order = done.shape[1], done.shape[2]
    others = [i for i in range(slabs) if i != c]

    def write(i):
        return pltpu.make_async_copy(done.at[:, i], out.at[:, i], sem.at[0])

    for i in others:
        write(i).start()
    high, low = split(arrived[c].reshape(2 * order, order))
    stacked = jnp.concatenate([high, high, low], axis=0)
    value[...] = jnp.dot(left[2], stacked, preferred_element_type=F32).reshape(2, order, order)
    write_last = pltpu.make_async_copy(value, out.at[:, c], sem.at[1])
    write_last.start()
    for i in others:
        write(i).wait()
    write_last.wait()


def fused(wide, narrow, amplitudes, gates):
    layout = amplitudes.shape
    slabs, order = layout[1], layout[4]
    vector = amplitudes.reshape(2, slabs, order, order)
    matrices = gates.reshape(6, 2, order, order)
    early = narrow == 4 and slabs == 8
    slots = slabs + early
    slab_buffer = pltpu.VMEM((slots, 2, order, order), F32)
    done, arrived, left = pl.pallas_call(
        functools.partial(kernel, wide, narrow, early),
        out_shape=[
            jax.ShapeDtypeStruct(vector.shape, F32),
            jax.ShapeDtypeStruct((slabs, 2, order, order), F32),
            jax.ShapeDtypeStruct((3, 2 * order, 6 * order), BF16),
        ],
        in_specs=[pl.BlockSpec(memory_space=pl.ANY)] * 2,
        out_specs=[pl.BlockSpec(memory_space=pltpu.VMEM)] * 3,
        scratch_shapes=[
            pltpu.VMEM((2, slots, order, order), F32),
            pltpu.VMEM(matrices.shape, F32),
            slab_buffer, slab_buffer, slab_buffer,
            pltpu.VMEM((6 * order, 2 * order), BF16),
            pltpu.SemaphoreType.REGULAR((wide + narrow - 2,)),
            pltpu.SemaphoreType.DMA((3,)),
            pltpu.SemaphoreType.DMA((2,)),
            pltpu.SemaphoreType.DMA((1,)),
            pltpu.SemaphoreType.DMA((slots,)),
            pltpu.SemaphoreType.DMA((1,)),
            pltpu.SemaphoreType.DMA((slabs - early,)),
            pltpu.SemaphoreType.DMA((2,)),
            pltpu.SemaphoreType.DMA((2,)),
        ],
        compiler_params=pltpu.CompilerParams(
            collective_id=0, has_side_effects=True, vmem_limit_bytes=24 << 20),
    )(*[pltpu.with_memory_space_constraint(value, pltpu.HBM) for value in (vector, matrices)])
    result = pl.pallas_call(
        functools.partial(finish, slabs - 1 - early),
        out_shape=jax.ShapeDtypeStruct(vector.shape, F32),
        in_specs=[pl.BlockSpec(memory_space=pltpu.VMEM)] * 3,
        out_specs=pl.BlockSpec(memory_space=pltpu.HBM),
        scratch_shapes=[
            pltpu.VMEM((2, order, order), F32),
            pltpu.SemaphoreType.DMA((2,)),
        ],
        compiler_params=pltpu.CompilerParams(vmem_limit_bytes=8 << 20),
    )(done, arrived, left)
    return result.reshape(layout)


def tiled(order, count):
    return count > 1 and count & (count - 1) == 0 and order % (8 * count) == 0


def solution(mesh):
    wide, narrow = mesh.shape["wide"], mesh.shape["narrow"]

    def shards(amplitudes, gates):
        order, slabs = amplitudes.shape[4], amplitudes.shape[1]
        if tiled(order, wide) and tiled(order, narrow) and wide * narrow <= 128 and slabs > 2:
            return fused(wide, narrow, amplitudes, gates)
        return plain(amplitudes, gates)

    return jax.shard_map(
        shards,
        mesh=mesh,
        in_specs=(P(None, None, "wide", "narrow", None, None), P()),
        out_specs=P(None, None, "wide", "narrow", None, None),
        check_vma=False,
    )
```

```python
import functools

import jax
import jax.numpy as jnp
from jax import lax
from jax.experimental import pallas as pl
from jax.experimental.pallas import tpu as pltpu
from jax.sharding import PartitionSpec as P

precise = lax.Precision.HIGHEST
MESH = pl.DeviceIdType.MESH
F32 = jnp.float32
BF16 = jnp.bfloat16
EARLY_AT = 5
DEFER_AT = 4
AHEAD = 3


def blocks(matrix):
    return jnp.stack([jnp.stack([matrix[0], -matrix[1]]), jnp.stack([matrix[1], matrix[0]])])


def on_rows(vector, matrix):
    return jnp.einsum("cdjk,drkb->crjb", blocks(matrix), vector, precision=precise)


def on_columns(vector, matrix):
    return jnp.einsum("cdjk,drak->craj", blocks(matrix), vector, precision=precise)


def plain(amplitudes, gates):
    layout = amplitudes.shape
    slabs, order = layout[1], layout[4]
    vector = amplitudes.reshape(2, slabs, order, order)
    vector = on_columns(on_rows(vector, gates[0, 0]), gates[0, 1])
    vector = lax.all_to_all(vector.reshape(layout), "wide", split_axis=4, concat_axis=2, tiled=True)
    vector = vector.reshape(2, slabs, order, order)
    vector = on_columns(on_rows(vector, gates[1, 0]), gates[1, 1])
    vector = lax.all_to_all(vector.reshape(layout), "narrow", split_axis=4, concat_axis=3, tiled=True)
    vector = vector.reshape(2, slabs, order, order)
    vector = on_columns(on_rows(vector, gates[2, 0]), gates[2, 1])
    return vector.reshape(layout)


def partner(me, mask, count):
    out, bit = 0, 1
    while bit < count:
        digit = me // bit % 2
        if mask & bit:
            digit = 1 - digit
        out = out + digit * bit
        bit *= 2
    return out


def far_first(count):
    return sorted(range(1, count), key=lambda m: (-bin(m >> 1).count("1"), -m))


def turn(w, count):
    if count != 8:
        return w
    chip = w // 2
    return 2 * (chip % 2 + chip // 2) + 1 - w % 2


def greeters(w, count):
    if count != 8:
        return w
    level = turn(w, count) // 2
    return level * (level + 1) + 1 - w % 2


def split(value):
    high = value.astype(BF16)
    return high, (value - high.astype(F32)).astype(BF16)


def real_form(matrix):
    re, im = matrix[0], matrix[1]
    return jnp.concatenate(
        [jnp.concatenate([re, -im], axis=1), jnp.concatenate([im, re], axis=1)], axis=0
    )


def kernel(wide, narrow, early, amp, gates, out, zr, left, x, g, y, yr, z, right,
           met, x_sem, g_sem, ws_sem, wr_sem, ns_sem, nr_sem, es_sem, er_sem):
    slabs, order = amp.shape[1], amp.shape[2]
    last = slabs - 1
    hw, hn = order // wide, order // narrow
    w, n = lax.axis_index("wide"), lax.axis_index("narrow")
    wide_masks = far_first(wide)
    narrow_masks = list(range(1, narrow))

    def wait(ref, sem):
        pltpu.make_async_copy(ref, ref, sem).wait()

    def load(i):
        part = [pl.ds(0, 1), pl.ds(last, 1), pl.ds(1, slabs - 2)][i]
        return pltpu.make_async_copy(amp.at[:, part], x.at[:, part], x_sem.at[i])

    def load_gate(i):
        part = pl.ds(0, 1) if i == 0 else pl.ds(1, 5)
        return pltpu.make_async_copy(gates.at[part], g.at[part], g_sem.at[i])

    def apart(mask):
        if wide != 8 or mask < 6:
            return False
        return turn(w, wide) // 2 == 1

    def comes_first(there, mask):
        return (turn(there, wide) < turn(w, wide)) & jnp.logical_not(apart(mask))

    def follows(there, mask):
        return (turn(there, wide) > turn(w, wide)) & jnp.logical_not(apart(mask))

    def hurried(here, there):
        return (here == 2) & (there == 1) if early else False

    def greet(after):
        for mask in wide_masks:
            there = partner(w, mask, wide)

            @pl.when(comes_first(there, mask) if not after else follows(there, mask))
            def _():
                sem = pltpu.get_barrier_semaphore() if after else met.at[mask - 1]
                pl.semaphore_signal(sem, inc=1, device_id=(there, n), device_id_type=MESH)
        for mask in narrow_masks:
            there = partner(n, mask, narrow)

            @pl.when((there > n) | hurried(n, there) if after else (there < n) & jnp.logical_not(hurried(n, there)))
            def _():
                sem = pltpu.get_barrier_semaphore() if after else met.at[wide + mask - 2]
                pl.semaphore_signal(sem, inc=1, device_id=(w, there), device_id_type=MESH)

    def send_wide(c, i):
        there = partner(w, wide_masks[i], wide)
        return pltpu.make_async_remote_copy(
            src_ref=y.at[c, :, pl.ds(pl.multiple_of(there * hw, hw), hw), :],
            dst_ref=yr.at[c, :, pl.ds(pl.multiple_of(w * hw, hw), hw), :],
            send_sem=ws_sem.at[0], recv_sem=wr_sem.at[c],
            device_id=(there, n), device_id_type=MESH)

    def send_narrow(c, i):
        there = partner(n, narrow_masks[i], narrow)
        if narrow == 4:
            there = [partner(n, 1, narrow), 3 - 3 * (n // 2), 2 - n // 2][i]
        return pltpu.make_async_remote_copy(
            src_ref=z.at[c, :, pl.ds(pl.multiple_of(there * hn, hn), hn), :],
            dst_ref=zr.at[c, :, pl.ds(pl.multiple_of(n * hn, hn), hn), :],
            send_sem=ns_sem.at[0], recv_sem=nr_sem.at[c],
            device_id=(w, there), device_id_type=MESH)

    def send_early():
        return pltpu.make_async_remote_copy(
            src_ref=x.at[:, last], dst_ref=x.at[:, slabs],
            send_sem=es_sem.at[0], recv_sem=er_sem.at[0],
            device_id=(w, partner(n, 3, narrow)), device_id_type=MESH)

    def send_half(k):
        there = partner(n, 1, narrow)
        index = partner(n, 3 * k, narrow)
        return pltpu.make_async_remote_copy(
            src_ref=z.at[last + k, :, pl.ds(pl.multiple_of(there * hn, hn), hn), :],
            dst_ref=zr.at[last, :, pl.ds(pl.multiple_of(index * hn, hn), hn), :],
            send_sem=es_sem.at[1], recv_sem=er_sem.at[1],
            device_id=(w, there), device_id_type=MESH)

    def prepare(t):
        high, low = split(real_form(g[2 * t]))
        left[t] = jnp.concatenate([high, low, high], axis=1)

    def rows(t, value):
        high, low = split(value.reshape(2 * order, order))
        stacked = jnp.concatenate([high, high, low], axis=0)
        return jnp.dot(left[t], stacked, preferred_element_type=F32)

    def columns(value):
        high, low = split(jnp.concatenate([value[:order], value[order:]], axis=1))
        stacked = jnp.concatenate([high, low, high], axis=1)
        return jnp.dot(stacked, right[...], preferred_element_type=F32)

    def first(c):
        y[c] = rows(0, x[:, c]).reshape(2, order, order)

    def answered(mask):
        @pl.when(follows(partner(w, mask, wide), mask))
        def _():
            pl.semaphore_wait(met.at[mask - 1], 1)

    def start_wide_known(c, known):
        def send_to(mask, when):
            @pl.when(when(partner(w, mask, wide), mask))
            def _():
                send_wide(c, wide_masks.index(mask)).start()

        def apart_last():
            for mask in wide_masks[::-1]:
                answered(mask)
            for mask in (4, 5, 7, 6, 3, 2, 1):
                if mask < 6:
                    send_to(mask, follows)
                else:
                    send_wide(c, wide_masks.index(mask)).start()

        def as_answered():
            for mask in wide_masks[::-1]:
                answered(mask)
                send_to(mask, follows)

        if known:
            for mask in wide_masks:
                send_to(mask, comes_first)
        elif wide == 8:
            pl.when(apart(6))(apart_last)
            pl.when(jnp.logical_not(apart(6)))(as_answered)
        else:
            as_answered()

    def start_wide(c):
        for i in range(wide - 1):
            send_wide(c, i).start()

    def second(c, with_columns, to):
        own = pl.ds(pl.multiple_of(w * hw, hw), hw)
        yr[c, :, own, :] = y[c, :, own, :]
        wait(yr.at[c, :, pl.ds(0, hw * (wide - 1)), :], wr_sem.at[c])
        value = rows(1, yr[c])
        if with_columns:
            value = columns(value)
            z[c, 0] = value[:, :order]
            z[c, 1] = value[:, order:]
        else:
            z[c] = value.reshape(2, order, order)
        for i in to:
            send_narrow(c, i).start()

    def start_ahead(c):
        if isinstance(c, int):
            if c + AHEAD < slabs:
                first(c + AHEAD)
                start_wide(c + AHEAD)
        else:
            @pl.when(c + AHEAD < slabs)
            def _():
                first(c + AHEAD)
                start_wide(c + AHEAD)

    def exchanged(c):
        own = pl.ds(pl.multiple_of(n * hn, hn), hn)
        zr[c, :, own, :] = z[c, :, own, :]
        wait(zr.at[c, :, pl.ds(0, hn * (narrow - 1)), :], nr_sem.at[c])

    def third(c, with_columns, whole=False):
        if not whole:
            exchanged(c)
        value = rows(2, zr[c])
        if with_columns:
            value = columns(value)
            out[0, c] = value[:, :order]
            out[1, c] = value[:, order:]
        else:
            out[0, c] = value[:order]
            out[1, c] = value[order:]

    load(1).start()
    load_gate(0).start()
    load(0).start()
    greet(True)
    load(2).start()
    load_gate(1).start()
    def meet():
        expected = greeters(w, wide) + n + jnp.where(n == 1, 1, 0) if early else greeters(w, wide) + n
        @pl.when(expected > 0)
        def _():
            pl.semaphore_wait(pltpu.get_barrier_semaphore(), expected)
        load(1).wait()
        if early:
            @pl.when(n > 0)
            def _():
                send_early().start()
        greet(False)

    pl.when(n != 1)(meet) if early else meet()
    load_gate(0).wait()
    prepare(0)
    load(0).wait()
    first(0)
    if early:
        pl.when(n == 1)(meet)
    start_wide_known(0, True)
    load(2).wait()
    first(1)
    start_wide_known(0, False)
    load_gate(1).wait()
    product = g[1].reshape(2 * order, order)
    for t in (1, 2):
        product = jnp.dot(real_form(g[2 * t + 1]), product, precision=precise, preferred_element_type=F32)
    re, im = product[:order].T, product[order:].T
    high, low = split(jnp.concatenate(
        [jnp.concatenate([re, im], axis=1), jnp.concatenate([-im, re], axis=1)], axis=0))
    right[...] = jnp.concatenate([high, high, low], axis=0)
    prepare(1)
    prepare(2)
    start_wide(1)
    if early:
        @pl.when(n == 0)
        def _():
            pl.semaphore_wait(met.at[wide + 1], 1)
            send_early().start()
    @pl.loop(2, AHEAD)
    def _(c):
        first(c)
        start_wide(c)

    for mask in narrow_masks:
        if not (early and mask == 3):
            @pl.when(partner(n, mask, narrow) > n)
            def _():
                pl.semaphore_wait(met.at[wide + mask - 2], 1)

    everywhere = list(range(narrow - 1))
    if early:
        soon, later = everywhere[:-1], everywhere[-1:]
        second(0, False, everywhere)
        start_ahead(0)

        @pl.loop(1, DEFER_AT)
        def _(c):
            second(c, True, everywhere)
            start_ahead(c)

        @pl.loop(DEFER_AT, EARLY_AT)
        def _(c):
            second(c, True, soon)
            start_ahead(c)

        send_early().wait_recv()
        first(slabs)
        start_wide(slabs)

        @pl.loop(EARLY_AT, last - 1)
        def _(c):
            second(c, True, soon)

        @pl.loop(last, slabs + 1)
        def _(c):
            second(c, False, [])

        for k in range(2):
            send_half(k).start()
            index = partner(n, 3 * k, narrow)
            rows_to = pl.ds(pl.multiple_of(index * hn, hn), hn)
            rows_from = pl.ds(pl.multiple_of(n * hn, hn), hn)
            zr[last, :, rows_to, :] = z[last + k, :, rows_from, :]

        second(last - 1, True, soon)

        @pl.loop(DEFER_AT, last)
        def _(c):
            for i in later:
                send_narrow(c, i).start()
    else:
        second(0, False, everywhere)
        start_ahead(0)

        @pl.loop(1, slabs)
        def _(c):
            second(c, True, everywhere)
            start_ahead(c)

    third(0, True)
    if early:
        @pl.loop(1, last - 1)
        def _(c):
            third(c, False)

        wait(zr.at[last, :, pl.ds(0, 2 * hn), :], er_sem.at[1])
        third(last, True, True)
        exchanged(last - 1)
    else:
        @pl.loop(1, last)
        def _(c):
            third(c, False)

        exchanged(last)

    wait(y.at[:, :, pl.ds(0, hw * (wide - 1)), :], ws_sem.at[0])
    wait(z.at[pl.ds(0, last if early else slabs), :, pl.ds(0, hn * (narrow - 1)), :], ns_sem.at[0])
    if early:
        send_early().wait_send()
        wait(z.at[last, :, pl.ds(0, 2 * hn), :], es_sem.at[1])


def finish(c, done, arrived, left, out, value, sem):
    slabs, order = done.shape[1], done.shape[2]
    others = [i for i in range(slabs) if i != c]

    def write(i):
        return pltpu.make_async_copy(done.at[:, i], out.at[:, i], sem.at[0])

    for i in others:
        write(i).start()
    high, low = split(arrived[c].reshape(2 * order, order))
    stacked = jnp.concatenate([high, high, low], axis=0)
    value[...] = jnp.dot(left[2], stacked, preferred_element_type=F32).reshape(2, order, order)
    write_last = pltpu.make_async_copy(value, out.at[:, c], sem.at[1])
    write_last.start()
    for i in others:
        write(i).wait()
    write_last.wait()


def fused(wide, narrow, amplitudes, gates):
    layout = amplitudes.shape
    slabs, order = layout[1], layout[4]
    vector = amplitudes.reshape(2, slabs, order, order)
    matrices = gates.reshape(6, 2, order, order)
    early = narrow == 4 and slabs == 8
    slots = slabs + early
    slab_buffer = pltpu.VMEM((slots, 2, order, order), F32)
    done, arrived, left = pl.pallas_call(
        functools.partial(kernel, wide, narrow, early),
        out_shape=[
            jax.ShapeDtypeStruct(vector.shape, F32),
            jax.ShapeDtypeStruct((slabs, 2, order, order), F32),
            jax.ShapeDtypeStruct((3, 2 * order, 6 * order), BF16),
        ],
        in_specs=[pl.BlockSpec(memory_space=pl.ANY)] * 2,
        out_specs=[pl.BlockSpec(memory_space=pltpu.VMEM)] * 3,
        scratch_shapes=[
            pltpu.VMEM((2, slots, order, order), F32),
            pltpu.VMEM(matrices.shape, F32),
            slab_buffer, slab_buffer, slab_buffer,
            pltpu.VMEM((6 * order, 2 * order), BF16),
            pltpu.SemaphoreType.REGULAR((wide + narrow - 2,)),
            pltpu.SemaphoreType.DMA((3,)),
            pltpu.SemaphoreType.DMA((2,)),
            pltpu.SemaphoreType.DMA((1,)),
            pltpu.SemaphoreType.DMA((slots,)),
            pltpu.SemaphoreType.DMA((1,)),
            pltpu.SemaphoreType.DMA((slabs - early,)),
            pltpu.SemaphoreType.DMA((2,)),
            pltpu.SemaphoreType.DMA((2,)),
        ],
        compiler_params=pltpu.CompilerParams(
            collective_id=0, has_side_effects=True, vmem_limit_bytes=24 << 20),
    )(*[pltpu.with_memory_space_constraint(value, pltpu.HBM) for value in (vector, matrices)])
    result = pl.pallas_call(
        functools.partial(finish, slabs - 1 - early),
        out_shape=jax.ShapeDtypeStruct(vector.shape, F32),
        in_specs=[pl.BlockSpec(memory_space=pltpu.VMEM)] * 3,
        out_specs=pl.BlockSpec(memory_space=pltpu.HBM),
        scratch_shapes=[
            pltpu.VMEM((2, order, order), F32),
            pltpu.SemaphoreType.DMA((2,)),
        ],
        compiler_params=pltpu.CompilerParams(vmem_limit_bytes=8 << 20),
    )(done, arrived, left)
    return result.reshape(layout)


def tiled(order, count):
    return count > 1 and count & (count - 1) == 0 and order % (8 * count) == 0


def solution(mesh):
    wide, narrow = mesh.shape["wide"], mesh.shape["narrow"]

    def shards(amplitudes, gates):
        order, slabs = amplitudes.shape[4], amplitudes.shape[1]
        if tiled(order, wide) and tiled(order, narrow) and wide * narrow <= 128 and slabs > 2:
            return fused(wide, narrow, amplitudes, gates)
        return plain(amplitudes, gates)

    return jax.shard_map(
        shards,
        mesh=mesh,
        in_specs=(P(None, None, "wide", "narrow", None, None), P()),
        out_specs=P(None, None, "wide", "narrow", None, None),
        check_vma=False,
    )
```

```python
import functools

import jax
import jax.numpy as jnp
from jax import lax
from jax.experimental import pallas as pl
from jax.experimental.pallas import tpu as pltpu
from jax.sharding import PartitionSpec as P

precise = lax.Precision.HIGHEST
MESH = pl.DeviceIdType.MESH
F32 = jnp.float32
BF16 = jnp.bfloat16
EARLY_AT = 5
DEFER_AT = 4
AHEAD = 3


def blocks(matrix):
    return jnp.stack([jnp.stack([matrix[0], -matrix[1]]), jnp.stack([matrix[1], matrix[0]])])


def on_rows(vector, matrix):
    return jnp.einsum("cdjk,drkb->crjb", blocks(matrix), vector, precision=precise)


def on_columns(vector, matrix):
    return jnp.einsum("cdjk,drak->craj", blocks(matrix), vector, precision=precise)


def plain(amplitudes, gates):
    layout = amplitudes.shape
    slabs, order = layout[1], layout[4]
    vector = amplitudes.reshape(2, slabs, order, order)
    vector = on_columns(on_rows(vector, gates[0, 0]), gates[0, 1])
    vector = lax.all_to_all(vector.reshape(layout), "wide", split_axis=4, concat_axis=2, tiled=True)
    vector = vector.reshape(2, slabs, order, order)
    vector = on_columns(on_rows(vector, gates[1, 0]), gates[1, 1])
    vector = lax.all_to_all(vector.reshape(layout), "narrow", split_axis=4, concat_axis=3, tiled=True)
    vector = vector.reshape(2, slabs, order, order)
    vector = on_columns(on_rows(vector, gates[2, 0]), gates[2, 1])
    return vector.reshape(layout)


def partner(me, mask, count):
    out, bit = 0, 1
    while bit < count:
        digit = me // bit % 2
        if mask & bit:
            digit = 1 - digit
        out = out + digit * bit
        bit *= 2
    return out


def far_first(count):
    return sorted(range(1, count), key=lambda m: (-bin(m >> 1).count("1"), -m))


def turn(w, count):
    if count != 8:
        return w
    chip = w // 2
    return 2 * (chip % 2 + chip // 2) + 1 - w % 2


def greeters(w, count):
    if count != 8:
        return w
    level = turn(w, count) // 2
    return level * (level + 1) + 1 - w % 2


def split(value):
    high = value.astype(BF16)
    return high, (value - high.astype(F32)).astype(BF16)


def real_form(matrix):
    re, im = matrix[0], matrix[1]
    return jnp.concatenate(
        [jnp.concatenate([re, -im], axis=1), jnp.concatenate([im, re], axis=1)], axis=0
    )


def kernel(wide, narrow, early, amp, gates, out, zr, left, x, g, y, yr, z, right,
           met, load_sem, ws_sem, wr_sem, ns_sem, nr_sem, er_sem):
    slabs, order = amp.shape[1], amp.shape[2]
    last = slabs - 1
    hw, hn = order // wide, order // narrow
    w, n = lax.axis_index("wide"), lax.axis_index("narrow")
    wide_masks = far_first(wide)
    narrow_masks = list(range(1, narrow))

    def wait(ref, sem):
        pltpu.make_async_copy(ref, ref, sem).wait()

    def load(i):
        part = [pl.ds(0, 1), pl.ds(last, 1), pl.ds(1, slabs - 2)][i]
        return pltpu.make_async_copy(amp.at[:, part], x.at[:, part], load_sem.at[i])

    def load_gate(i):
        part = pl.ds(0, 1) if i == 0 else pl.ds(1, 5)
        return pltpu.make_async_copy(gates.at[part], g.at[part], load_sem.at[3 * i])

    def apart(mask):
        if wide != 8 or mask < 6:
            return False
        return turn(w, wide) // 2 == 1

    def comes_first(there, mask):
        return (turn(there, wide) < turn(w, wide)) & jnp.logical_not(apart(mask))

    def follows(there, mask):
        return (turn(there, wide) > turn(w, wide)) & jnp.logical_not(apart(mask))

    def wide_met(mask):
        return 2 + max(mask.bit_length() - 2, 0) + (mask >= 6) if wide == 8 else 2

    def narrow_met(mask):
        return 1 if early and mask == 3 else 0

    def hurried(here, there):
        return (here == 2) & (there == 1) if early else False

    def greet(after):
        for mask in wide_masks:
            there = partner(w, mask, wide)

            @pl.when(comes_first(there, mask) if not after else follows(there, mask))
            def _():
                sem = pltpu.get_barrier_semaphore() if after else met.at[wide_met(mask)]
                pl.semaphore_signal(sem, inc=1, device_id=(there, n), device_id_type=MESH)
        for mask in narrow_masks:
            there = partner(n, mask, narrow)

            @pl.when((there > n) | hurried(n, there) if after else (there < n) & jnp.logical_not(hurried(n, there)))
            def _():
                sem = pltpu.get_barrier_semaphore() if after else met.at[narrow_met(mask)]
                pl.semaphore_signal(sem, inc=1, device_id=(w, there), device_id_type=MESH)

    def wide_slot(c):
        return c - jnp.where(c == slabs, 1, 0) if early else c

    def send_wide(c, i):
        there = partner(w, wide_masks[i], wide)
        return pltpu.make_async_remote_copy(
            src_ref=y.at[c, :, pl.ds(pl.multiple_of(there * hw, hw), hw), :],
            dst_ref=yr.at[c, :, pl.ds(pl.multiple_of(w * hw, hw), hw), :],
            send_sem=ws_sem.at[0], recv_sem=wr_sem.at[wide_slot(c)],
            device_id=(there, n), device_id_type=MESH)

    def send_narrow(c, i):
        there = partner(n, narrow_masks[i], narrow)
        if narrow == 4:
            there = [partner(n, 1, narrow), 3 - 3 * (n // 2), 2 - n // 2][i]
        return pltpu.make_async_remote_copy(
            src_ref=z.at[c, :, pl.ds(pl.multiple_of(there * hn, hn), hn), :],
            dst_ref=zr.at[c, :, pl.ds(pl.multiple_of(n * hn, hn), hn), :],
            send_sem=ns_sem.at[0], recv_sem=nr_sem.at[c // 2],
            device_id=(w, there), device_id_type=MESH)

    def send_early():
        return pltpu.make_async_remote_copy(
            src_ref=x.at[:, last], dst_ref=x.at[:, slabs],
            send_sem=ns_sem.at[0], recv_sem=er_sem.at[0],
            device_id=(w, partner(n, 3, narrow)), device_id_type=MESH)

    def send_half(k):
        there = partner(n, 1, narrow)
        index = partner(n, 3 * k, narrow)
        return pltpu.make_async_remote_copy(
            src_ref=z.at[last + k, :, pl.ds(pl.multiple_of(there * hn, hn), hn), :],
            dst_ref=zr.at[last, :, pl.ds(pl.multiple_of(index * hn, hn), hn), :],
            send_sem=ns_sem.at[0], recv_sem=er_sem.at[1],
            device_id=(w, there), device_id_type=MESH)

    def prepare(t):
        high, low = split(real_form(g[2 * t]))
        left[t] = jnp.concatenate([high, low, high], axis=1)

    def rows(t, value):
        high, low = split(value.reshape(2 * order, order))
        stacked = jnp.concatenate([high, high, low], axis=0)
        return jnp.dot(left[t], stacked, preferred_element_type=F32)

    def columns(value):
        high, low = split(jnp.concatenate([value[:order], value[order:]], axis=1))
        stacked = jnp.concatenate([high, low, high], axis=1)
        return jnp.dot(stacked, right[...], preferred_element_type=F32)

    def first(c):
        y[c] = rows(0, x[:, c]).reshape(2, order, order)

    def answered(masks):
        count = sum(jnp.where(follows(partner(w, mask, wide), mask), 1, 0) for mask in masks)

        @pl.when(count > 0)
        def _():
            pl.semaphore_wait(met.at[wide_met(masks[0])], count)

    def start_wide_known(c, known):
        def send_to(mask, when):
            @pl.when(when(partner(w, mask, wide), mask))
            def _():
                send_wide(c, wide_masks.index(mask)).start()

        groups = [(1, 2, 3), (4, 5), (6, 7)] if wide == 8 else [wide_masks[::-1]]

        def apart_last():
            for masks in groups:
                answered(masks)
            for mask in (4, 5, 7, 6, 3, 2, 1):
                if mask < 6:
                    send_to(mask, follows)
                else:
                    send_wide(c, wide_masks.index(mask)).start()

        def as_answered():
            for masks in groups:
                answered(masks)
                for mask in masks:
                    send_to(mask, follows)

        if known:
            for mask in wide_masks:
                send_to(mask, comes_first)
        elif wide == 8:
            pl.when(apart(6))(apart_last)
            pl.when(jnp.logical_not(apart(6)))(as_answered)
        else:
            as_answered()

    def start_wide(c):
        for i in range(wide - 1):
            send_wide(c, i).start()

    def second(c, with_columns, to, awaited=1):
        own = pl.ds(pl.multiple_of(w * hw, hw), hw)
        yr[c, :, own, :] = y[c, :, own, :]
        if awaited:
            wait(yr.at[pl.ds(c, awaited), :, pl.ds(0, hw * (wide - 1)), :], wr_sem.at[wide_slot(c)])
        value = rows(1, yr[c])
        if with_columns:
            value = columns(value)
            z[c, 0] = value[:, :order]
            z[c, 1] = value[:, order:]
        else:
            z[c] = value.reshape(2, order, order)
        for i in to:
            send_narrow(c, i).start()

    def start_ahead(c):
        if isinstance(c, int):
            if c + AHEAD < slabs:
                first(c + AHEAD)
                start_wide(c + AHEAD)
        else:
            @pl.when(c + AHEAD < slabs)
            def _():
                first(c + AHEAD)
                start_wide(c + AHEAD)

    def exchanged(c, awaited):
        own = pl.ds(pl.multiple_of(n * hn, hn), hn)
        zr[c, :, own, :] = z[c, :, own, :]
        if awaited:
            wait(zr.at[pl.ds(c, awaited), :, pl.ds(0, hn * (narrow - 1)), :], nr_sem.at[c // 2])

    def third(c, with_columns, awaited=None):
        if awaited is not None:
            exchanged(c, awaited)
        value = rows(2, zr[c])
        if with_columns:
            value = columns(value)
            out[0, c] = value[:, :order]
            out[1, c] = value[:, order:]
        else:
            out[0, c] = value[:order]
            out[1, c] = value[order:]

    load(1).start()
    load_gate(0).start()
    load(0).start()
    greet(True)
    load(2).start()
    load_gate(1).start()
    def meet():
        expected = greeters(w, wide) + n + jnp.where(n == 1, 1, 0) if early else greeters(w, wide) + n
        @pl.when(expected > 0)
        def _():
            pl.semaphore_wait(pltpu.get_barrier_semaphore(), expected)
        load(1).wait()
        if early:
            @pl.when(n > 0)
            def _():
                send_early().start()
        greet(False)

    pl.when(n != 1)(meet) if early else meet()
    wait(g.at[pl.ds(0, 2)], load_sem.at[0])
    prepare(0)
    first(0)
    if early:
        pl.when(n == 1)(meet)
    start_wide_known(0, True)
    load(2).wait()
    first(1)
    start_wide_known(0, False)
    load_gate(1).wait()
    product = g[1].reshape(2 * order, order)
    for t in (1, 2):
        product = jnp.dot(real_form(g[2 * t + 1]), product, precision=precise, preferred_element_type=F32)
    re, im = product[:order].T, product[order:].T
    high, low = split(jnp.concatenate(
        [jnp.concatenate([re, im], axis=1), jnp.concatenate([-im, re], axis=1)], axis=0))
    right[...] = jnp.concatenate([high, high, low], axis=0)
    prepare(1)
    prepare(2)
    start_wide(1)
    if early:
        @pl.when(n == 0)
        def _():
            pl.semaphore_wait(met.at[1], 1)
            send_early().start()
    @pl.loop(2, AHEAD)
    def _(c):
        first(c)
        start_wide(c)

    later_ones = [mask for mask in narrow_masks if narrow_met(mask) == 0]
    count = sum(jnp.where(partner(n, mask, narrow) > n, 1, 0) for mask in later_ones)

    @pl.when(count > 0)
    def _():
        pl.semaphore_wait(met.at[0], count)

    everywhere = list(range(narrow - 1))
    if early:
        soon, later = everywhere[:-1], everywhere[-1:]
        second(0, False, everywhere)
        start_ahead(0)

        @pl.loop(1, DEFER_AT)
        def _(c):
            second(c, True, everywhere)
            start_ahead(c)

        @pl.loop(DEFER_AT, EARLY_AT)
        def _(c):
            second(c, True, soon)
            start_ahead(c)

        send_early().wait_recv()
        first(slabs)
        start_wide(slabs)

        @pl.loop(EARLY_AT, last - 1)
        def _(c):
            second(c, True, soon)

        second(last, False, [], 2)
        second(slabs, False, [], 0)

        for k in range(2):
            send_half(k).start()
            index = partner(n, 3 * k, narrow)
            rows_to = pl.ds(pl.multiple_of(index * hn, hn), hn)
            rows_from = pl.ds(pl.multiple_of(n * hn, hn), hn)
            zr[last, :, rows_to, :] = z[last + k, :, rows_from, :]

        second(last - 1, True, soon)

        @pl.loop(DEFER_AT, last)
        def _(c):
            for i in later:
                send_narrow(c, i).start()
    else:
        second(0, False, everywhere)
        start_ahead(0)

        @pl.loop(1, slabs)
        def _(c):
            second(c, True, everywhere)
            start_ahead(c)

    def third_last():
        wait(zr.at[last, :, pl.ds(0, 2 * hn), :], er_sem.at[1])
        third(last, True)

    third(0, True, 2)
    third(1, False, 0)
    middle = (n == 1) | (n == 2)
    if early:
        pl.when(middle)(third_last)

    @pl.loop(1, (slabs - 1) // 2)
    def _(p):
        third(2 * p, False, 2)
        third(2 * p + 1, False, 0)

    if early:
        pl.when(jnp.logical_not(middle))(third_last)
    if early:
        exchanged(last - 1, 1)
    else:
        if slabs % 2 == 0:
            third(last - 1, False, 2)
        exchanged(last, 1 if slabs % 2 else 0)

    wait(y.at[:, :, pl.ds(0, hw * (wide - 1)), :], ws_sem.at[0])
    wait(z.at[:, :, pl.ds(0, hn * (narrow - 1)), :], ns_sem.at[0])


def finish(c, done, arrived, left, out, value, sem):
    slabs, order = done.shape[1], done.shape[2]
    others = [i for i in range(slabs) if i != c]

    def write(i):
        return pltpu.make_async_copy(done.at[:, i], out.at[:, i], sem.at[0])

    for i in others:
        write(i).start()
    high, low = split(arrived[c].reshape(2 * order, order))
    stacked = jnp.concatenate([high, high, low], axis=0)
    value[...] = jnp.dot(left[2], stacked, preferred_element_type=F32).reshape(2, order, order)
    write_last = pltpu.make_async_copy(value, out.at[:, c], sem.at[1])
    write_last.start()
    for i in others:
        write(i).wait()
    write_last.wait()


def fused(wide, narrow, amplitudes, gates):
    layout = amplitudes.shape
    slabs, order = layout[1], layout[4]
    vector = amplitudes.reshape(2, slabs, order, order)
    matrices = gates.reshape(6, 2, order, order)
    early = narrow == 4 and slabs == 8
    slots = slabs + early
    slab_buffer = pltpu.VMEM((slots, 2, order, order), F32)
    done, arrived, left = pl.pallas_call(
        functools.partial(kernel, wide, narrow, early),
        out_shape=[
            jax.ShapeDtypeStruct(vector.shape, F32),
            jax.ShapeDtypeStruct((slabs, 2, order, order), F32),
            jax.ShapeDtypeStruct((3, 2 * order, 6 * order), BF16),
        ],
        in_specs=[pl.BlockSpec(memory_space=pl.ANY)] * 2,
        out_specs=[pl.BlockSpec(memory_space=pltpu.VMEM)] * 3,
        scratch_shapes=[
            pltpu.VMEM((2, slots, order, order), F32),
            pltpu.VMEM(matrices.shape, F32),
            slab_buffer, slab_buffer, slab_buffer,
            pltpu.VMEM((6 * order, 2 * order), BF16),
            pltpu.SemaphoreType.REGULAR((5,)),
            pltpu.SemaphoreType.DMA((4,)),
            pltpu.SemaphoreType.DMA((1,)),
            pltpu.SemaphoreType.DMA((slabs,)),
            pltpu.SemaphoreType.DMA((1,)),
            pltpu.SemaphoreType.DMA(((slabs + 1 - early) // 2,)),
            pltpu.SemaphoreType.DMA((1 + early,)),
        ],
        compiler_params=pltpu.CompilerParams(
            collective_id=0, has_side_effects=True, vmem_limit_bytes=24 << 20),
    )(*[pltpu.with_memory_space_constraint(value, pltpu.HBM) for value in (vector, matrices)])
    result = pl.pallas_call(
        functools.partial(finish, slabs - 1 - early),
        out_shape=jax.ShapeDtypeStruct(vector.shape, F32),
        in_specs=[pl.BlockSpec(memory_space=pltpu.VMEM)] * 3,
        out_specs=pl.BlockSpec(memory_space=pltpu.HBM),
        scratch_shapes=[
            pltpu.VMEM((2, order, order), F32),
            pltpu.SemaphoreType.DMA((2,)),
        ],
        compiler_params=pltpu.CompilerParams(vmem_limit_bytes=8 << 20),
    )(done, arrived, left)
    return result.reshape(layout)


def tiled(order, count):
    return count > 1 and count & (count - 1) == 0 and order % (8 * count) == 0


def solution(mesh):
    wide, narrow = mesh.shape["wide"], mesh.shape["narrow"]

    def shards(amplitudes, gates):
        order, slabs = amplitudes.shape[4], amplitudes.shape[1]
        if tiled(order, wide) and tiled(order, narrow) and wide * narrow <= 128 and slabs > 2:
            return fused(wide, narrow, amplitudes, gates)
        return plain(amplitudes, gates)

    return jax.shard_map(
        shards,
        mesh=mesh,
        in_specs=(P(None, None, "wide", "narrow", None, None), P()),
        out_specs=P(None, None, "wide", "narrow", None, None),
        check_vma=False,
    )
```

```python
import functools

import jax
import jax.numpy as jnp
from jax import lax
from jax.experimental import pallas as pl
from jax.experimental.pallas import tpu as pltpu
from jax.sharding import PartitionSpec as P

precise = lax.Precision.HIGHEST
MESH = pl.DeviceIdType.MESH
F32 = jnp.float32
BF16 = jnp.bfloat16
EARLY_AT = 4
DEFER_AT = 4
AHEAD = 3


def blocks(matrix):
    return jnp.stack([jnp.stack([matrix[0], -matrix[1]]), jnp.stack([matrix[1], matrix[0]])])


def on_rows(vector, matrix):
    return jnp.einsum("cdjk,drkb->crjb", blocks(matrix), vector, precision=precise)


def on_columns(vector, matrix):
    return jnp.einsum("cdjk,drak->craj", blocks(matrix), vector, precision=precise)


def plain(amplitudes, gates):
    layout = amplitudes.shape
    slabs, order = layout[1], layout[4]
    vector = amplitudes.reshape(2, slabs, order, order)
    vector = on_columns(on_rows(vector, gates[0, 0]), gates[0, 1])
    vector = lax.all_to_all(vector.reshape(layout), "wide", split_axis=4, concat_axis=2, tiled=True)
    vector = vector.reshape(2, slabs, order, order)
    vector = on_columns(on_rows(vector, gates[1, 0]), gates[1, 1])
    vector = lax.all_to_all(vector.reshape(layout), "narrow", split_axis=4, concat_axis=3, tiled=True)
    vector = vector.reshape(2, slabs, order, order)
    vector = on_columns(on_rows(vector, gates[2, 0]), gates[2, 1])
    return vector.reshape(layout)


def partner(me, mask, count):
    out, bit = 0, 1
    while bit < count:
        digit = me // bit % 2
        if mask & bit:
            digit = 1 - digit
        out = out + digit * bit
        bit *= 2
    return out


def far_first(count):
    return sorted(range(1, count), key=lambda m: (-bin(m >> 1).count("1"), -m))


def turn(w, count):
    if count != 8:
        return w
    chip = w // 2
    return 2 * (chip % 2 + chip // 2) + 1 - w % 2


def greeters(w, count):
    if count != 8:
        return w
    level = turn(w, count) // 2
    return level * (level + 1) + 1 - w % 2


def split(value):
    high = value.astype(BF16)
    return high, (value - high.astype(F32)).astype(BF16)


def real_form(matrix):
    re, im = matrix[0], matrix[1]
    return jnp.concatenate(
        [jnp.concatenate([re, -im], axis=1), jnp.concatenate([im, re], axis=1)], axis=0
    )


def kernel(wide, narrow, early, amp, gates, out, zr, left, x, g, y, yr, z, right,
           met, load_sem, ws_sem, wr_sem, ns_sem, nr_sem, er_sem):
    slabs, order = amp.shape[1], amp.shape[2]
    last = slabs - 1
    hw, hn = order // wide, order // narrow
    w, n = lax.axis_index("wide"), lax.axis_index("narrow")
    wide_masks = far_first(wide)
    narrow_masks = list(range(1, narrow))

    def wait(ref, sem):
        pltpu.make_async_copy(ref, ref, sem).wait()

    def load(i):
        part = [pl.ds(0, 1), pl.ds(last, 1), pl.ds(1, slabs - 2)][i]
        return pltpu.make_async_copy(amp.at[:, part], x.at[:, part], load_sem.at[i])

    def load_gate(i):
        part = pl.ds(0, 1) if i == 0 else pl.ds(1, 5)
        return pltpu.make_async_copy(gates.at[part], g.at[part], load_sem.at[3 * i])

    def apart(mask):
        if wide != 8 or mask < 6:
            return False
        return turn(w, wide) // 2 == 1

    def comes_first(there, mask):
        return (turn(there, wide) < turn(w, wide)) & jnp.logical_not(apart(mask))

    def follows(there, mask):
        return (turn(there, wide) > turn(w, wide)) & jnp.logical_not(apart(mask))

    def wide_met(mask):
        return 2 + max(mask.bit_length() - 2, 0) + (mask >= 6) if wide == 8 else 2

    def narrow_met(mask):
        return 1 if early and mask == 3 else 0

    def hurried(here, there):
        return (here == 2) & (there == 1) if early else False

    def greet(after):
        for mask in wide_masks:
            there = partner(w, mask, wide)

            @pl.when(comes_first(there, mask) if not after else follows(there, mask))
            def _():
                sem = pltpu.get_barrier_semaphore() if after else met.at[wide_met(mask)]
                pl.semaphore_signal(sem, inc=1, device_id=(there, n), device_id_type=MESH)
        for mask in narrow_masks:
            there = partner(n, mask, narrow)

            @pl.when((there > n) | hurried(n, there) if after else (there < n) & jnp.logical_not(hurried(n, there)))
            def _():
                sem = pltpu.get_barrier_semaphore() if after else met.at[narrow_met(mask)]
                pl.semaphore_signal(sem, inc=1, device_id=(w, there), device_id_type=MESH)

    def wide_slot(c):
        return c - jnp.where(c == slabs, 1, 0) if early else c

    def narrow_slot(c):
        return jnp.where(c < DEFER_AT, c // 2, c - DEFER_AT // 2) if early else c

    def send_wide(c, i):
        there = partner(w, wide_masks[i], wide)
        return pltpu.make_async_remote_copy(
            src_ref=y.at[c, :, pl.ds(pl.multiple_of(there * hw, hw), hw), :],
            dst_ref=yr.at[c, :, pl.ds(pl.multiple_of(w * hw, hw), hw), :],
            send_sem=ws_sem.at[0], recv_sem=wr_sem.at[wide_slot(c)],
            device_id=(there, n), device_id_type=MESH)

    def send_narrow(c, i):
        there = partner(n, narrow_masks[i], narrow)
        if narrow == 4:
            there = [partner(n, 1, narrow), 3 - 3 * (n // 2), 2 - n // 2][i]
        return pltpu.make_async_remote_copy(
            src_ref=z.at[c, :, pl.ds(pl.multiple_of(there * hn, hn), hn), :],
            dst_ref=zr.at[c, :, pl.ds(pl.multiple_of(n * hn, hn), hn), :],
            send_sem=ns_sem.at[0], recv_sem=nr_sem.at[narrow_slot(c)],
            device_id=(w, there), device_id_type=MESH)

    def send_early():
        return pltpu.make_async_remote_copy(
            src_ref=x.at[:, last], dst_ref=x.at[:, slabs],
            send_sem=ns_sem.at[0], recv_sem=er_sem.at[0],
            device_id=(w, partner(n, 3, narrow)), device_id_type=MESH)

    def send_half(k):
        there = partner(n, 1, narrow)
        index = partner(n, 3 * k, narrow)
        return pltpu.make_async_remote_copy(
            src_ref=z.at[last + k, :, pl.ds(pl.multiple_of(there * hn, hn), hn), :],
            dst_ref=zr.at[last, :, pl.ds(pl.multiple_of(index * hn, hn), hn), :],
            send_sem=ns_sem.at[0], recv_sem=er_sem.at[1],
            device_id=(w, there), device_id_type=MESH)

    def prepare(t):
        high, low = split(real_form(g[2 * t]))
        left[t] = jnp.concatenate([high, low, high], axis=1)

    def rows(t, value):
        high, low = split(value.reshape(2 * order, order))
        stacked = jnp.concatenate([high, high, low], axis=0)
        return jnp.dot(left[t], stacked, preferred_element_type=F32)

    def columns(value):
        high, low = split(jnp.concatenate([value[:order], value[order:]], axis=1))
        stacked = jnp.concatenate([high, low, high], axis=1)
        return jnp.dot(stacked, right[...], preferred_element_type=F32)

    def first(c):
        y[c] = rows(0, x[:, c]).reshape(2, order, order)

    def answered(masks):
        count = sum(jnp.where(follows(partner(w, mask, wide), mask), 1, 0) for mask in masks)

        @pl.when(count > 0)
        def _():
            pl.semaphore_wait(met.at[wide_met(masks[0])], count)

    def start_wide_known(c, known):
        def send_to(mask, when):
            @pl.when(when(partner(w, mask, wide), mask))
            def _():
                send_wide(c, wide_masks.index(mask)).start()

        groups = [(1, 2, 3), (4, 5), (6, 7)] if wide == 8 else [wide_masks[::-1]]

        def apart_last():
            for masks in groups:
                answered(masks)
            for mask in (4, 5, 7, 6, 3, 2, 1):
                if mask < 6:
                    send_to(mask, follows)
                else:
                    send_wide(c, wide_masks.index(mask)).start()

        def as_answered():
            for masks in groups:
                answered(masks)
                for mask in masks:
                    send_to(mask, follows)

        if known:
            for mask in wide_masks:
                send_to(mask, comes_first)
        elif wide == 8:
            pl.when(apart(6))(apart_last)
            pl.when(jnp.logical_not(apart(6)))(as_answered)
        else:
            as_answered()

    def start_wide(c):
        for i in range(wide - 1):
            send_wide(c, i).start()

    def second(c, with_columns, to, awaited=1):
        own = pl.ds(pl.multiple_of(w * hw, hw), hw)
        yr[c, :, own, :] = y[c, :, own, :]
        if awaited:
            wait(yr.at[pl.ds(c, awaited), :, pl.ds(0, hw * (wide - 1)), :], wr_sem.at[wide_slot(c)])
        value = rows(1, yr[c])
        if with_columns:
            value = columns(value)
            z[c, 0] = value[:, :order]
            z[c, 1] = value[:, order:]
        else:
            z[c] = value.reshape(2, order, order)
        for i in to:
            send_narrow(c, i).start()

    def start_ahead(c):
        if isinstance(c, int):
            if c + AHEAD < slabs:
                first(c + AHEAD)
                start_wide(c + AHEAD)
        else:
            @pl.when(c + AHEAD < slabs)
            def _():
                first(c + AHEAD)
                start_wide(c + AHEAD)

    def exchanged(c, awaited):
        own = pl.ds(pl.multiple_of(n * hn, hn), hn)
        zr[c, :, own, :] = z[c, :, own, :]
        if awaited:
            wait(zr.at[pl.ds(c, awaited), :, pl.ds(0, hn * (narrow - 1)), :], nr_sem.at[narrow_slot(c)])

    def third(c, with_columns, awaited=None):
        if awaited is not None:
            exchanged(c, awaited)
        value = rows(2, zr[c])
        if with_columns:
            value = columns(value)
            out[0, c] = value[:, :order]
            out[1, c] = value[:, order:]
        else:
            out[0, c] = value[:order]
            out[1, c] = value[order:]

    load(1).start()
    load_gate(0).start()
    load(0).start()
    greet(True)
    load(2).start()
    load_gate(1).start()
    def meet():
        expected = greeters(w, wide) + n + jnp.where(n == 1, 1, 0) if early else greeters(w, wide) + n
        @pl.when(expected > 0)
        def _():
            pl.semaphore_wait(pltpu.get_barrier_semaphore(), expected)
        load(1).wait()
        if early:
            @pl.when(n > 0)
            def _():
                send_early().start()
        greet(False)

    pl.when(n != 1)(meet) if early else meet()
    wait(g.at[pl.ds(0, 2)], load_sem.at[0])
    prepare(0)
    first(0)
    if early:
        pl.when(n == 1)(meet)
    start_wide_known(0, True)
    load(2).wait()
    first(1)
    start_wide_known(0, False)
    load_gate(1).wait()
    product = g[1].reshape(2 * order, order)
    for t in (1, 2):
        product = jnp.dot(real_form(g[2 * t + 1]), product, precision=precise, preferred_element_type=F32)
    re, im = product[:order].T, product[order:].T
    high, low = split(jnp.concatenate(
        [jnp.concatenate([re, im], axis=1), jnp.concatenate([-im, re], axis=1)], axis=0))
    right[...] = jnp.concatenate([high, high, low], axis=0)
    prepare(1)
    prepare(2)
    start_wide(1)
    if early:
        @pl.when(n == 0)
        def _():
            pl.semaphore_wait(met.at[1], 1)
            send_early().start()
    @pl.loop(2, AHEAD)
    def _(c):
        first(c)
        start_wide(c)

    later_ones = [mask for mask in narrow_masks if narrow_met(mask) == 0]
    count = sum(jnp.where(partner(n, mask, narrow) > n, 1, 0) for mask in later_ones)

    @pl.when(count > 0)
    def _():
        pl.semaphore_wait(met.at[0], count)

    everywhere = list(range(narrow - 1))
    if early:
        soon, later = everywhere[:-1], everywhere[-1:]
        second(0, False, everywhere)
        start_ahead(0)

        @pl.loop(1, DEFER_AT)
        def _(c):
            second(c, True, everywhere)
            start_ahead(c)

        @pl.loop(DEFER_AT, EARLY_AT)
        def _(c):
            second(c, True, soon)
            start_ahead(c)

        send_early().wait_recv()
        first(slabs)
        start_wide(slabs)

        @pl.loop(EARLY_AT, last - 1)
        def _(c):
            second(c, True, soon)
            start_ahead(c)

        second(last, False, [], 2)
        second(slabs, False, [], 0)

        for k in range(2):
            send_half(k).start()
            index = partner(n, 3 * k, narrow)
            rows_to = pl.ds(pl.multiple_of(index * hn, hn), hn)
            rows_from = pl.ds(pl.multiple_of(n * hn, hn), hn)
            zr[last, :, rows_to, :] = z[last + k, :, rows_from, :]

        second(last - 1, True, soon)

        @pl.loop(DEFER_AT, last)
        def _(c):
            for i in later:
                send_narrow(c, i).start()
    else:
        second(0, False, everywhere)
        start_ahead(0)

        @pl.loop(1, slabs)
        def _(c):
            second(c, True, everywhere)
            start_ahead(c)

    def third_last():
        wait(zr.at[last, :, pl.ds(0, 2 * hn), :], er_sem.at[1])
        third(last, True)

    middle = (n == 1) | (n == 2)
    if early:
        third(0, True, 2)
        third(1, False, 0)
        pl.when(middle)(third_last)

        @pl.loop(1, DEFER_AT // 2)
        def _(p):
            third(2 * p, False, 2)
            third(2 * p + 1, False, 0)

        @pl.loop(DEFER_AT, last - 1)
        def _(c):
            third(c, False, 1)

        pl.when(jnp.logical_not(middle))(third_last)
        exchanged(last - 1, 1)
    else:
        third(0, True, 1)

        @pl.loop(1, last)
        def _(c):
            third(c, False, 1)

        exchanged(last, 1)

    wait(y.at[:, :, pl.ds(0, hw * (wide - 1)), :], ws_sem.at[0])
    wait(z.at[:, :, pl.ds(0, hn * (narrow - 1)), :], ns_sem.at[0])


def finish(c, done, arrived, left, out, value, sem):
    slabs, order = done.shape[1], done.shape[2]
    others = [i for i in range(slabs) if i != c]

    def write(i):
        return pltpu.make_async_copy(done.at[:, i], out.at[:, i], sem.at[0])

    for i in others:
        write(i).start()
    high, low = split(arrived[c].reshape(2 * order, order))
    stacked = jnp.concatenate([high, high, low], axis=0)
    value[...] = jnp.dot(left[2], stacked, preferred_element_type=F32).reshape(2, order, order)
    write_last = pltpu.make_async_copy(value, out.at[:, c], sem.at[1])
    write_last.start()
    for i in others:
        write(i).wait()
    write_last.wait()


def fused(wide, narrow, amplitudes, gates):
    layout = amplitudes.shape
    slabs, order = layout[1], layout[4]
    vector = amplitudes.reshape(2, slabs, order, order)
    matrices = gates.reshape(6, 2, order, order)
    early = narrow == 4 and slabs == 8
    slots = slabs + early
    slab_buffer = pltpu.VMEM((slots, 2, order, order), F32)
    done, arrived, left = pl.pallas_call(
        functools.partial(kernel, wide, narrow, early),
        out_shape=[
            jax.ShapeDtypeStruct(vector.shape, F32),
            jax.ShapeDtypeStruct((slabs, 2, order, order), F32),
            jax.ShapeDtypeStruct((3, 2 * order, 6 * order), BF16),
        ],
        in_specs=[pl.BlockSpec(memory_space=pl.ANY)] * 2,
        out_specs=[pl.BlockSpec(memory_space=pltpu.VMEM)] * 3,
        scratch_shapes=[
            pltpu.VMEM((2, slots, order, order), F32),
            pltpu.VMEM(matrices.shape, F32),
            slab_buffer, slab_buffer, slab_buffer,
            pltpu.VMEM((6 * order, 2 * order), BF16),
            pltpu.SemaphoreType.REGULAR((5,)),
            pltpu.SemaphoreType.DMA((4,)),
            pltpu.SemaphoreType.DMA((1,)),
            pltpu.SemaphoreType.DMA((slabs,)),
            pltpu.SemaphoreType.DMA((1,)),
            pltpu.SemaphoreType.DMA((slabs - 1 - DEFER_AT // 2 if early else slabs,)),
            pltpu.SemaphoreType.DMA((1 + early,)),
        ],
        compiler_params=pltpu.CompilerParams(
            collective_id=0, has_side_effects=True, vmem_limit_bytes=24 << 20),
    )(*[pltpu.with_memory_space_constraint(value, pltpu.HBM) for value in (vector, matrices)])
    result = pl.pallas_call(
        functools.partial(finish, slabs - 1 - early),
        out_shape=jax.ShapeDtypeStruct(vector.shape, F32),
        in_specs=[pl.BlockSpec(memory_space=pltpu.VMEM)] * 3,
        out_specs=pl.BlockSpec(memory_space=pltpu.HBM),
        scratch_shapes=[
            pltpu.VMEM((2, order, order), F32),
            pltpu.SemaphoreType.DMA((2,)),
        ],
        compiler_params=pltpu.CompilerParams(vmem_limit_bytes=8 << 20),
    )(done, arrived, left)
    return result.reshape(layout)


def tiled(order, count):
    return count > 1 and count & (count - 1) == 0 and order % (8 * count) == 0


def solution(mesh):
    wide, narrow = mesh.shape["wide"], mesh.shape["narrow"]

    def shards(amplitudes, gates):
        order, slabs = amplitudes.shape[4], amplitudes.shape[1]
        if tiled(order, wide) and tiled(order, narrow) and wide * narrow <= 128 and slabs > 2:
            return fused(wide, narrow, amplitudes, gates)
        return plain(amplitudes, gates)

    return jax.shard_map(
        shards,
        mesh=mesh,
        in_specs=(P(None, None, "wide", "narrow", None, None), P()),
        out_specs=P(None, None, "wide", "narrow", None, None),
        check_vma=False,
    )
```

```python
import functools

import jax
import jax.numpy as jnp
from jax import lax
from jax.experimental import pallas as pl
from jax.experimental.pallas import tpu as pltpu
from jax.sharding import PartitionSpec as P

precise = lax.Precision.HIGHEST
MESH = pl.DeviceIdType.MESH
F32 = jnp.float32
BF16 = jnp.bfloat16
EARLY_AT = 4
DEFER_AT = 4
AHEAD = 3


def blocks(matrix):
    return jnp.stack([jnp.stack([matrix[0], -matrix[1]]), jnp.stack([matrix[1], matrix[0]])])


def on_rows(vector, matrix):
    return jnp.einsum("cdjk,drkb->crjb", blocks(matrix), vector, precision=precise)


def on_columns(vector, matrix):
    return jnp.einsum("cdjk,drak->craj", blocks(matrix), vector, precision=precise)


def plain(amplitudes, gates):
    layout = amplitudes.shape
    slabs, order = layout[1], layout[4]
    vector = amplitudes.reshape(2, slabs, order, order)
    vector = on_columns(on_rows(vector, gates[0, 0]), gates[0, 1])
    vector = lax.all_to_all(vector.reshape(layout), "wide", split_axis=4, concat_axis=2, tiled=True)
    vector = vector.reshape(2, slabs, order, order)
    vector = on_columns(on_rows(vector, gates[1, 0]), gates[1, 1])
    vector = lax.all_to_all(vector.reshape(layout), "narrow", split_axis=4, concat_axis=3, tiled=True)
    vector = vector.reshape(2, slabs, order, order)
    vector = on_columns(on_rows(vector, gates[2, 0]), gates[2, 1])
    return vector.reshape(layout)


def partner(me, mask, count):
    out, bit = 0, 1
    while bit < count:
        digit = me // bit % 2
        if mask & bit:
            digit = 1 - digit
        out = out + digit * bit
        bit *= 2
    return out


def far_first(count):
    return sorted(range(1, count), key=lambda m: (-bin(m >> 1).count("1"), -m))


def turn(w, count):
    if count != 8:
        return w
    chip = w // 2
    return 2 * (chip % 2 + chip // 2) + 1 - w % 2


def greeters(w, count):
    if count != 8:
        return w
    level = turn(w, count) // 2
    return level * (level + 1) + 1 - w % 2


def split(value):
    high = value.astype(BF16)
    return high, (value - high.astype(F32)).astype(BF16)


def real_form(matrix):
    re, im = matrix[0], matrix[1]
    return jnp.concatenate(
        [jnp.concatenate([re, -im], axis=1), jnp.concatenate([im, re], axis=1)], axis=0
    )


def kernel(wide, narrow, early, amp, gates, out, zr, left, x, g, y, yr, z, right,
           met, load_sem, ws_sem, wr_sem, ns_sem, nr_sem, er_sem):
    slabs, order = amp.shape[1], amp.shape[2]
    last = slabs - 1
    hw, hn = order // wide, order // narrow
    w, n = lax.axis_index("wide"), lax.axis_index("narrow")
    wide_masks = far_first(wide)
    narrow_masks = list(range(1, narrow))

    def wait(ref, sem):
        pltpu.make_async_copy(ref, ref, sem).wait()

    def load(i):
        part = [pl.ds(0, 1), pl.ds(last, 1), pl.ds(1, slabs - 2)][i]
        return pltpu.make_async_copy(amp.at[:, part], x.at[:, part], load_sem.at[i])

    def load_last(k):
        return pltpu.make_async_copy(amp.at[k, last], x.at[k, last], load_sem.at[1 + 3 * k])

    def load_gate(i):
        part = pl.ds(0, 1) if i == 0 else pl.ds(1, 5)
        return pltpu.make_async_copy(gates.at[part], g.at[part], load_sem.at[3 * i])

    def apart(mask):
        if wide != 8 or mask < 6:
            return False
        return turn(w, wide) // 2 == 1

    def comes_first(there, mask):
        return (turn(there, wide) < turn(w, wide)) & jnp.logical_not(apart(mask))

    def follows(there, mask):
        return (turn(there, wide) > turn(w, wide)) & jnp.logical_not(apart(mask))

    def wide_met(mask):
        return 2 + max(mask.bit_length() - 2, 0) + (mask >= 6) if wide == 8 else 2

    def narrow_met(mask):
        return 1 if early and mask == 3 else 0

    def hurried(here, there):
        return (here == 2) & (there == 1) if early else False

    def greet(after):
        for mask in wide_masks:
            there = partner(w, mask, wide)

            @pl.when(comes_first(there, mask) if not after else follows(there, mask))
            def _():
                sem = pltpu.get_barrier_semaphore() if after else met.at[wide_met(mask)]
                pl.semaphore_signal(sem, inc=1, device_id=(there, n), device_id_type=MESH)
        for mask in narrow_masks:
            there = partner(n, mask, narrow)

            @pl.when((there > n) | hurried(n, there) if after else (there < n) & jnp.logical_not(hurried(n, there)))
            def _():
                sem = pltpu.get_barrier_semaphore() if after else met.at[narrow_met(mask)]
                pl.semaphore_signal(sem, inc=1, device_id=(w, there), device_id_type=MESH)

    def wide_slot(c):
        return c - jnp.where(c == slabs, 1, 0) if early else c

    def narrow_slot(c):
        return jnp.where(c < DEFER_AT, c // 2, c - DEFER_AT // 2) if early else c

    def send_wide(c, i):
        there = partner(w, wide_masks[i], wide)
        return pltpu.make_async_remote_copy(
            src_ref=y.at[c, :, pl.ds(pl.multiple_of(there * hw, hw), hw), :],
            dst_ref=yr.at[c, :, pl.ds(pl.multiple_of(w * hw, hw), hw), :],
            send_sem=ws_sem.at[0], recv_sem=wr_sem.at[wide_slot(c)],
            device_id=(there, n), device_id_type=MESH)

    def send_narrow(c, i):
        there = partner(n, narrow_masks[i], narrow)
        if narrow == 4:
            there = [partner(n, 1, narrow), 3 - 3 * (n // 2), 2 - n // 2][i]
        return pltpu.make_async_remote_copy(
            src_ref=z.at[c, :, pl.ds(pl.multiple_of(there * hn, hn), hn), :],
            dst_ref=zr.at[c, :, pl.ds(pl.multiple_of(n * hn, hn), hn), :],
            send_sem=ns_sem.at[0], recv_sem=nr_sem.at[narrow_slot(c)],
            device_id=(w, there), device_id_type=MESH)

    def send_early(k):
        return pltpu.make_async_remote_copy(
            src_ref=x.at[k, last], dst_ref=x.at[k, slabs],
            send_sem=ns_sem.at[0], recv_sem=er_sem.at[0],
            device_id=(w, partner(n, 3, narrow)), device_id_type=MESH)

    def send_half(k):
        there = partner(n, 1, narrow)
        index = partner(n, 3 * k, narrow)
        return pltpu.make_async_remote_copy(
            src_ref=z.at[last + k, :, pl.ds(pl.multiple_of(there * hn, hn), hn), :],
            dst_ref=zr.at[last, :, pl.ds(pl.multiple_of(index * hn, hn), hn), :],
            send_sem=ns_sem.at[0], recv_sem=er_sem.at[1],
            device_id=(w, there), device_id_type=MESH)

    def prepare(t):
        high, low = split(real_form(g[2 * t]))
        left[t] = jnp.concatenate([high, low, high], axis=1)

    def rows(t, value):
        high, low = split(value.reshape(2 * order, order))
        stacked = jnp.concatenate([high, high, low], axis=0)
        return jnp.dot(left[t], stacked, preferred_element_type=F32)

    def columns(value):
        high, low = split(jnp.concatenate([value[:order], value[order:]], axis=1))
        stacked = jnp.concatenate([high, low, high], axis=1)
        return jnp.dot(stacked, right[...], preferred_element_type=F32)

    def first(c):
        y[c] = rows(0, x[:, c]).reshape(2, order, order)

    def answered(masks):
        count = sum(jnp.where(follows(partner(w, mask, wide), mask), 1, 0) for mask in masks)

        @pl.when(count > 0)
        def _():
            pl.semaphore_wait(met.at[wide_met(masks[0])], count)

    def start_wide_known(c, known):
        def send_to(mask, when):
            @pl.when(when(partner(w, mask, wide), mask))
            def _():
                send_wide(c, wide_masks.index(mask)).start()

        groups = [(1, 2, 3), (4, 5), (6, 7)] if wide == 8 else [wide_masks[::-1]]

        def apart_last():
            for masks in groups:
                answered(masks)
            for mask in (4, 5, 7, 6, 3, 2, 1):
                if mask < 6:
                    send_to(mask, follows)
                else:
                    send_wide(c, wide_masks.index(mask)).start()

        def as_answered():
            for masks in groups:
                answered(masks)
                for mask in masks:
                    send_to(mask, follows)

        if known:
            for mask in wide_masks:
                send_to(mask, comes_first)
        elif wide == 8:
            pl.when(apart(6))(apart_last)
            pl.when(jnp.logical_not(apart(6)))(as_answered)
        else:
            as_answered()

    def start_wide(c):
        for i in range(wide - 1):
            send_wide(c, i).start()

    def second(c, with_columns, to, awaited=1):
        own = pl.ds(pl.multiple_of(w * hw, hw), hw)
        yr[c, :, own, :] = y[c, :, own, :]
        if awaited:
            wait(yr.at[pl.ds(c, awaited), :, pl.ds(0, hw * (wide - 1)), :], wr_sem.at[wide_slot(c)])
        value = rows(1, yr[c])
        if with_columns:
            value = columns(value)
            z[c, 0] = value[:, :order]
            z[c, 1] = value[:, order:]
        else:
            z[c] = value.reshape(2, order, order)
        for i in to:
            send_narrow(c, i).start()

    def start_ahead(c):
        if isinstance(c, int):
            if c + AHEAD < slabs:
                first(c + AHEAD)
                start_wide(c + AHEAD)
        else:
            @pl.when(c + AHEAD < slabs)
            def _():
                first(c + AHEAD)
                start_wide(c + AHEAD)

    def exchanged(c, awaited):
        own = pl.ds(pl.multiple_of(n * hn, hn), hn)
        zr[c, :, own, :] = z[c, :, own, :]
        if awaited:
            wait(zr.at[pl.ds(c, awaited), :, pl.ds(0, hn * (narrow - 1)), :], nr_sem.at[narrow_slot(c)])

    def third(c, with_columns, awaited=None):
        if awaited is not None:
            exchanged(c, awaited)
        value = rows(2, zr[c])
        if with_columns:
            value = columns(value)
            out[0, c] = value[:, :order]
            out[1, c] = value[:, order:]
        else:
            out[0, c] = value[:order]
            out[1, c] = value[order:]

    for k in range(2):
        load_last(k).start()
    load_gate(0).start()
    load(0).start()
    greet(True)
    load(2).start()
    load_gate(1).start()
    def meet():
        expected = greeters(w, wide) + n + jnp.where(n == 1, 1, 0) if early else greeters(w, wide) + n
        @pl.when(expected > 0)
        def _():
            pl.semaphore_wait(pltpu.get_barrier_semaphore(), expected)
        for k in range(2):
            load_last(k).wait()
            if early:
                @pl.when(n > 0)
                def _():
                    send_early(k).start()
        greet(False)

    pl.when(n != 1)(meet) if early else meet()
    wait(g.at[pl.ds(0, 2)], load_sem.at[0])
    prepare(0)
    first(0)
    if early:
        pl.when(n == 1)(meet)
    start_wide_known(0, True)
    load(2).wait()
    first(1)
    start_wide_known(0, False)
    load_gate(1).wait()
    product = g[1].reshape(2 * order, order)
    for t in (1, 2):
        product = jnp.dot(real_form(g[2 * t + 1]), product, precision=precise, preferred_element_type=F32)
    re, im = product[:order].T, product[order:].T
    high, low = split(jnp.concatenate(
        [jnp.concatenate([re, im], axis=1), jnp.concatenate([-im, re], axis=1)], axis=0))
    right[...] = jnp.concatenate([high, high, low], axis=0)
    prepare(1)
    prepare(2)
    start_wide(1)
    if early:
        @pl.when(n == 0)
        def _():
            pl.semaphore_wait(met.at[1], 1)
            for k in range(2):
                send_early(k).start()
    @pl.loop(2, AHEAD)
    def _(c):
        first(c)
        start_wide(c)

    later_ones = [mask for mask in narrow_masks if narrow_met(mask) == 0]
    count = sum(jnp.where(partner(n, mask, narrow) > n, 1, 0) for mask in later_ones)

    @pl.when(count > 0)
    def _():
        pl.semaphore_wait(met.at[0], count)

    everywhere = list(range(narrow - 1))
    if early:
        soon, later = everywhere[:-1], everywhere[-1:]
        second(0, False, everywhere)
        start_ahead(0)

        @pl.loop(1, DEFER_AT)
        def _(c):
            second(c, True, everywhere)
            start_ahead(c)

        @pl.loop(DEFER_AT, EARLY_AT)
        def _(c):
            second(c, True, soon)
            start_ahead(c)

        wait(x.at[:, slabs], er_sem.at[0])
        first(slabs)
        start_wide(slabs)

        @pl.loop(EARLY_AT, last - 1)
        def _(c):
            second(c, True, soon)
            start_ahead(c)

        second(last, False, [], 2)
        second(slabs, False, [], 0)

        for k in range(2):
            send_half(k).start()
            index = partner(n, 3 * k, narrow)
            rows_to = pl.ds(pl.multiple_of(index * hn, hn), hn)
            rows_from = pl.ds(pl.multiple_of(n * hn, hn), hn)
            zr[last, :, rows_to, :] = z[last + k, :, rows_from, :]

        second(last - 1, True, soon)

        @pl.loop(DEFER_AT, last)
        def _(c):
            for i in later:
                send_narrow(c, i).start()
    else:
        second(0, False, everywhere)
        start_ahead(0)

        @pl.loop(1, slabs)
        def _(c):
            second(c, True, everywhere)
            start_ahead(c)

    def third_last():
        wait(zr.at[last, :, pl.ds(0, 2 * hn), :], er_sem.at[1])
        third(last, True)

    middle = (n == 1) | (n == 2)
    if early:
        third(0, True, 2)
        third(1, False, 0)
        pl.when(middle)(third_last)

        @pl.loop(1, DEFER_AT // 2)
        def _(p):
            third(2 * p, False, 2)
            third(2 * p + 1, False, 0)

        @pl.loop(DEFER_AT, last - 1)
        def _(c):
            third(c, False, 1)

        pl.when(jnp.logical_not(middle))(third_last)
        exchanged(last - 1, 1)
    else:
        third(0, True, 1)

        @pl.loop(1, last)
        def _(c):
            third(c, False, 1)

        exchanged(last, 1)

    wait(y.at[:, :, pl.ds(0, hw * (wide - 1)), :], ws_sem.at[0])
    wait(z.at[:, :, pl.ds(0, hn * (narrow - 1)), :], ns_sem.at[0])


def finish(c, done, arrived, left, out, value, sem):
    slabs, order = done.shape[1], done.shape[2]
    others = [i for i in range(slabs) if i != c]

    def write(i):
        return pltpu.make_async_copy(done.at[:, i], out.at[:, i], sem.at[0])

    for i in others:
        write(i).start()
    high, low = split(arrived[c].reshape(2 * order, order))
    stacked = jnp.concatenate([high, high, low], axis=0)
    value[...] = jnp.dot(left[2], stacked, preferred_element_type=F32).reshape(2, order, order)
    write_last = pltpu.make_async_copy(value, out.at[:, c], sem.at[1])
    write_last.start()
    for i in others:
        write(i).wait()
    write_last.wait()


def fused(wide, narrow, amplitudes, gates):
    layout = amplitudes.shape
    slabs, order = layout[1], layout[4]
    vector = amplitudes.reshape(2, slabs, order, order)
    matrices = gates.reshape(6, 2, order, order)
    early = narrow == 4 and slabs == 8
    slots = slabs + early
    slab_buffer = pltpu.VMEM((slots, 2, order, order), F32)
    done, arrived, left = pl.pallas_call(
        functools.partial(kernel, wide, narrow, early),
        out_shape=[
            jax.ShapeDtypeStruct(vector.shape, F32),
            jax.ShapeDtypeStruct((slabs, 2, order, order), F32),
            jax.ShapeDtypeStruct((3, 2 * order, 6 * order), BF16),
        ],
        in_specs=[pl.BlockSpec(memory_space=pl.ANY)] * 2,
        out_specs=[pl.BlockSpec(memory_space=pltpu.VMEM)] * 3,
        scratch_shapes=[
            pltpu.VMEM((2, slots, order, order), F32),
            pltpu.VMEM(matrices.shape, F32),
            slab_buffer, slab_buffer, slab_buffer,
            pltpu.VMEM((6 * order, 2 * order), BF16),
            pltpu.SemaphoreType.REGULAR((5,)),
            pltpu.SemaphoreType.DMA((5,)),
            pltpu.SemaphoreType.DMA((1,)),
            pltpu.SemaphoreType.DMA((slabs,)),
            pltpu.SemaphoreType.DMA((1,)),
            pltpu.SemaphoreType.DMA((slabs - 1 - DEFER_AT // 2 if early else slabs,)),
            pltpu.SemaphoreType.DMA((1 + early,)),
        ],
        compiler_params=pltpu.CompilerParams(
            collective_id=0, has_side_effects=True, vmem_limit_bytes=24 << 20),
    )(*[pltpu.with_memory_space_constraint(value, pltpu.HBM) for value in (vector, matrices)])
    result = pl.pallas_call(
        functools.partial(finish, slabs - 1 - early),
        out_shape=jax.ShapeDtypeStruct(vector.shape, F32),
        in_specs=[pl.BlockSpec(memory_space=pltpu.VMEM)] * 3,
        out_specs=pl.BlockSpec(memory_space=pltpu.HBM),
        scratch_shapes=[
            pltpu.VMEM((2, order, order), F32),
            pltpu.SemaphoreType.DMA((2,)),
        ],
        compiler_params=pltpu.CompilerParams(vmem_limit_bytes=8 << 20),
    )(done, arrived, left)
    return result.reshape(layout)


def tiled(order, count):
    return count > 1 and count & (count - 1) == 0 and order % (8 * count) == 0


def solution(mesh):
    wide, narrow = mesh.shape["wide"], mesh.shape["narrow"]

    def shards(amplitudes, gates):
        order, slabs = amplitudes.shape[4], amplitudes.shape[1]
        if tiled(order, wide) and tiled(order, narrow) and wide * narrow <= 128 and slabs > 2:
            return fused(wide, narrow, amplitudes, gates)
        return plain(amplitudes, gates)

    return jax.shard_map(
        shards,
        mesh=mesh,
        in_specs=(P(None, None, "wide", "narrow", None, None), P()),
        out_specs=P(None, None, "wide", "narrow", None, None),
        check_vma=False,
    )
```

```python
import functools

import jax
import jax.numpy as jnp
from jax import lax
from jax.experimental import pallas as pl
from jax.experimental.pallas import tpu as pltpu
from jax.sharding import PartitionSpec as P

precise = lax.Precision.HIGHEST
MESH = pl.DeviceIdType.MESH
F32 = jnp.float32
BF16 = jnp.bfloat16
EARLY_AT = 4
DEFER_AT = 4
AHEAD = 3


def blocks(matrix):
    return jnp.stack([jnp.stack([matrix[0], -matrix[1]]), jnp.stack([matrix[1], matrix[0]])])


def on_rows(vector, matrix):
    return jnp.einsum("cdjk,drkb->crjb", blocks(matrix), vector, precision=precise)


def on_columns(vector, matrix):
    return jnp.einsum("cdjk,drak->craj", blocks(matrix), vector, precision=precise)


def plain(amplitudes, gates):
    layout = amplitudes.shape
    slabs, order = layout[1], layout[4]
    vector = amplitudes.reshape(2, slabs, order, order)
    vector = on_columns(on_rows(vector, gates[0, 0]), gates[0, 1])
    vector = lax.all_to_all(vector.reshape(layout), "wide", split_axis=4, concat_axis=2, tiled=True)
    vector = vector.reshape(2, slabs, order, order)
    vector = on_columns(on_rows(vector, gates[1, 0]), gates[1, 1])
    vector = lax.all_to_all(vector.reshape(layout), "narrow", split_axis=4, concat_axis=3, tiled=True)
    vector = vector.reshape(2, slabs, order, order)
    vector = on_columns(on_rows(vector, gates[2, 0]), gates[2, 1])
    return vector.reshape(layout)


def partner(me, mask, count):
    out, bit = 0, 1
    while bit < count:
        digit = me // bit % 2
        if mask & bit:
            digit = 1 - digit
        out = out + digit * bit
        bit *= 2
    return out


def far_first(count):
    return sorted(range(1, count), key=lambda m: (-bin(m >> 1).count("1"), -m))


def turn(w, count):
    if count != 8:
        return w
    chip = w // 2
    return 2 * (chip % 2 + chip // 2) + 1 - w % 2


def greeters(w, count):
    if count != 8:
        return w
    level = turn(w, count) // 2
    return level * (level + 1) // (1 + w % 2) + 1 - w % 2


def split(value):
    high = value.astype(BF16)
    return high, (value - high.astype(F32)).astype(BF16)


def real_form(matrix):
    re, im = matrix[0], matrix[1]
    return jnp.concatenate(
        [jnp.concatenate([re, -im], axis=1), jnp.concatenate([im, re], axis=1)], axis=0
    )


def kernel(wide, narrow, early, amp, gates, out, zr, left, x, g, y, yr, z, right,
           met, load_sem, ws_sem, wr_sem, ns_sem, nr_sem, er_sem):
    slabs, order = amp.shape[1], amp.shape[2]
    last = slabs - 1
    hw, hn = order // wide, order // narrow
    w, n = lax.axis_index("wide"), lax.axis_index("narrow")
    wide_masks = far_first(wide)
    narrow_masks = list(range(1, narrow))

    def wait(ref, sem):
        pltpu.make_async_copy(ref, ref, sem).wait()

    def load(i):
        part = [pl.ds(0, 1), pl.ds(last, 1), pl.ds(1, slabs - 2)][i]
        return pltpu.make_async_copy(amp.at[:, part], x.at[:, part], load_sem.at[i])

    def load_last(k):
        return pltpu.make_async_copy(amp.at[k, last], x.at[k, last], load_sem.at[1 + 3 * k])

    def load_gate(i):
        part = pl.ds(0, 1) if i == 0 else pl.ds(1, 5)
        return pltpu.make_async_copy(gates.at[part], g.at[part], load_sem.at[3 * i])

    def apart(mask):
        if wide != 8 or mask < 6:
            return False
        return turn(w, wide) // 2 == 1

    def through_partner(near, far):
        return (near % 2 == 0) & (far % 2 == 1) & (turn(near, wide) // 2 < turn(far, wide) // 2) if wide == 8 else False

    def comes_first(there, mask):
        return (turn(there, wide) < turn(w, wide)) & jnp.logical_not(apart(mask)) & jnp.logical_not(through_partner(there, w))

    def follows(there, mask):
        return (turn(there, wide) > turn(w, wide)) & jnp.logical_not(apart(mask)) & jnp.logical_not(through_partner(w, there))

    def not_yet(there, mask):
        return jnp.logical_not(comes_first(there, mask))

    def wide_met(mask):
        return 2 + max(mask.bit_length() - 2, 0) + (mask >= 6) if wide == 8 else 2

    def narrow_met(mask):
        return 1 if early and mask == 3 else 0

    def hurried(here, there):
        return (here == 2) & (there == 1) if early else False

    def greet(after):
        for mask in wide_masks:
            there = partner(w, mask, wide)

            @pl.when(comes_first(there, mask) if not after else follows(there, mask))
            def _():
                sem = pltpu.get_barrier_semaphore() if after else met.at[wide_met(mask)]
                pl.semaphore_signal(sem, inc=1, device_id=(there, n), device_id_type=MESH)
        for mask in narrow_masks:
            there = partner(n, mask, narrow)

            @pl.when((there > n) | hurried(n, there) if after else (there < n) & jnp.logical_not(hurried(n, there)))
            def _():
                sem = pltpu.get_barrier_semaphore() if after else met.at[narrow_met(mask)]
                pl.semaphore_signal(sem, inc=1, device_id=(w, there), device_id_type=MESH)

    def wide_slot(c):
        return c - jnp.where(c == slabs, 1, 0) if early else c

    def narrow_slot(c):
        return jnp.where(c < DEFER_AT, c // 2, c - DEFER_AT // 2) if early else c

    def send_wide(c, i):
        there = partner(w, wide_masks[i], wide)
        return pltpu.make_async_remote_copy(
            src_ref=y.at[c, :, pl.ds(pl.multiple_of(there * hw, hw), hw), :],
            dst_ref=yr.at[c, :, pl.ds(pl.multiple_of(w * hw, hw), hw), :],
            send_sem=ws_sem.at[0], recv_sem=wr_sem.at[wide_slot(c)],
            device_id=(there, n), device_id_type=MESH)

    def send_narrow(c, i):
        there = partner(n, narrow_masks[i], narrow)
        if narrow == 4:
            there = [partner(n, 1, narrow), 3 - 3 * (n // 2), 2 - n // 2][i]
        return pltpu.make_async_remote_copy(
            src_ref=z.at[c, :, pl.ds(pl.multiple_of(there * hn, hn), hn), :],
            dst_ref=zr.at[c, :, pl.ds(pl.multiple_of(n * hn, hn), hn), :],
            send_sem=ns_sem.at[0], recv_sem=nr_sem.at[narrow_slot(c)],
            device_id=(w, there), device_id_type=MESH)

    def send_early(k):
        return pltpu.make_async_remote_copy(
            src_ref=x.at[k, last], dst_ref=x.at[k, slabs],
            send_sem=ns_sem.at[0], recv_sem=er_sem.at[0],
            device_id=(w, partner(n, 3, narrow)), device_id_type=MESH)

    def send_half(k):
        there = partner(n, 1, narrow)
        index = partner(n, 3 * k, narrow)
        return pltpu.make_async_remote_copy(
            src_ref=z.at[last + k, :, pl.ds(pl.multiple_of(there * hn, hn), hn), :],
            dst_ref=zr.at[last, :, pl.ds(pl.multiple_of(index * hn, hn), hn), :],
            send_sem=ns_sem.at[0], recv_sem=er_sem.at[1],
            device_id=(w, there), device_id_type=MESH)

    def prepare(t):
        high, low = split(real_form(g[2 * t]))
        left[t] = jnp.concatenate([high, low, high], axis=1)

    def rows(t, value):
        high, low = split(value.reshape(2 * order, order))
        stacked = jnp.concatenate([high, high, low], axis=0)
        return jnp.dot(left[t], stacked, preferred_element_type=F32)

    def columns(value):
        high, low = split(jnp.concatenate([value[:order], value[order:]], axis=1))
        stacked = jnp.concatenate([high, low, high], axis=1)
        return jnp.dot(stacked, right[...], preferred_element_type=F32)

    def first(c):
        y[c] = rows(0, x[:, c]).reshape(2, order, order)

    def answered(masks):
        count = sum(jnp.where(follows(partner(w, mask, wide), mask), 1, 0) for mask in masks)

        @pl.when(count > 0)
        def _():
            pl.semaphore_wait(met.at[wide_met(masks[0])], count)

    def start_wide_known(c, known):
        def send_to(mask, when):
            @pl.when(when(partner(w, mask, wide), mask))
            def _():
                send_wide(c, wide_masks.index(mask)).start()

        groups = [(1, 2, 3), (4, 5), (6, 7)] if wide == 8 else [wide_masks[::-1]]

        def apart_last():
            for masks in groups:
                answered(masks)
            for mask in (4, 5, 7, 6, 3, 2, 1):
                if mask < 6:
                    send_to(mask, not_yet)
                else:
                    send_wide(c, wide_masks.index(mask)).start()

        def as_answered():
            for masks in groups:
                answered(masks)
                for mask in masks:
                    send_to(mask, not_yet)

        if known:
            for mask in wide_masks:
                send_to(mask, comes_first)
        elif wide == 8:
            pl.when(apart(6))(apart_last)
            pl.when(jnp.logical_not(apart(6)))(as_answered)
        else:
            as_answered()

    def start_wide(c):
        for i in range(wide - 1):
            send_wide(c, i).start()

    def second(c, with_columns, to, awaited=1):
        own = pl.ds(pl.multiple_of(w * hw, hw), hw)
        yr[c, :, own, :] = y[c, :, own, :]
        if awaited:
            wait(yr.at[pl.ds(c, awaited), :, pl.ds(0, hw * (wide - 1)), :], wr_sem.at[wide_slot(c)])
        value = rows(1, yr[c])
        if with_columns:
            value = columns(value)
            z[c, 0] = value[:, :order]
            z[c, 1] = value[:, order:]
        else:
            z[c] = value.reshape(2, order, order)
        for i in to:
            send_narrow(c, i).start()

    def start_ahead(c):
        if isinstance(c, int):
            if c + AHEAD < slabs:
                first(c + AHEAD)
                start_wide(c + AHEAD)
        else:
            @pl.when(c + AHEAD < slabs)
            def _():
                first(c + AHEAD)
                start_wide(c + AHEAD)

    def exchanged(c, awaited):
        own = pl.ds(pl.multiple_of(n * hn, hn), hn)
        zr[c, :, own, :] = z[c, :, own, :]
        if awaited:
            wait(zr.at[pl.ds(c, awaited), :, pl.ds(0, hn * (narrow - 1)), :], nr_sem.at[narrow_slot(c)])

    def third(c, with_columns, awaited=None):
        if awaited is not None:
            exchanged(c, awaited)
        value = rows(2, zr[c])
        if with_columns:
            value = columns(value)
            out[0, c] = value[:, :order]
            out[1, c] = value[:, order:]
        else:
            out[0, c] = value[:order]
            out[1, c] = value[order:]

    for k in range(2):
        load_last(k).start()
    load_gate(0).start()
    load(0).start()
    greet(True)
    load(2).start()
    load_gate(1).start()
    def meet():
        expected = greeters(w, wide) + n + jnp.where(n == 1, 1, 0) if early else greeters(w, wide) + n
        @pl.when(expected > 0)
        def _():
            pl.semaphore_wait(pltpu.get_barrier_semaphore(), expected)
        for k in range(2):
            load_last(k).wait()
            if early:
                @pl.when(n > 0)
                def _():
                    send_early(k).start()
        greet(False)

    pl.when(n != 1)(meet) if early else meet()
    wait(g.at[pl.ds(0, 2)], load_sem.at[0])
    prepare(0)
    first(0)
    if early:
        pl.when(n == 1)(meet)
    start_wide_known(0, True)
    load(2).wait()
    first(1)
    start_wide_known(0, False)
    load_gate(1).wait()
    product = g[1].reshape(2 * order, order)
    for t in (1, 2):
        product = jnp.dot(real_form(g[2 * t + 1]), product, precision=precise, preferred_element_type=F32)
    re, im = product[:order].T, product[order:].T
    high, low = split(jnp.concatenate(
        [jnp.concatenate([re, im], axis=1), jnp.concatenate([-im, re], axis=1)], axis=0))
    right[...] = jnp.concatenate([high, high, low], axis=0)
    prepare(1)
    prepare(2)
    start_wide(1)
    if early:
        @pl.when(n == 0)
        def _():
            pl.semaphore_wait(met.at[1], 1)
            for k in range(2):
                send_early(k).start()
    @pl.loop(2, AHEAD)
    def _(c):
        first(c)
        start_wide(c)

    later_ones = [mask for mask in narrow_masks if narrow_met(mask) == 0]
    count = sum(jnp.where(partner(n, mask, narrow) > n, 1, 0) for mask in later_ones)

    @pl.when(count > 0)
    def _():
        pl.semaphore_wait(met.at[0], count)

    everywhere = list(range(narrow - 1))
    if early:
        soon, later = everywhere[:-1], everywhere[-1:]
        second(0, False, everywhere)
        start_ahead(0)

        @pl.loop(1, DEFER_AT)
        def _(c):
            second(c, True, everywhere)
            start_ahead(c)

        @pl.loop(DEFER_AT, EARLY_AT)
        def _(c):
            second(c, True, soon)
            start_ahead(c)

        wait(x.at[:, slabs], er_sem.at[0])
        first(slabs)
        start_wide(slabs)

        @pl.loop(EARLY_AT, last - 1)
        def _(c):
            second(c, True, soon)
            start_ahead(c)

        second(last, False, [], 2)
        second(slabs, False, [], 0)

        for k in range(2):
            send_half(k).start()
            index = partner(n, 3 * k, narrow)
            rows_to = pl.ds(pl.multiple_of(index * hn, hn), hn)
            rows_from = pl.ds(pl.multiple_of(n * hn, hn), hn)
            zr[last, :, rows_to, :] = z[last + k, :, rows_from, :]

        second(last - 1, True, soon)

        @pl.loop(DEFER_AT, last)
        def _(c):
            for i in later:
                send_narrow(c, i).start()
    else:
        second(0, False, everywhere)
        start_ahead(0)

        @pl.loop(1, slabs)
        def _(c):
            second(c, True, everywhere)
            start_ahead(c)

    def third_last():
        wait(zr.at[last, :, pl.ds(0, 2 * hn), :], er_sem.at[1])
        third(last, True)

    middle = (n == 1) | (n == 2)
    if early:
        third(0, True, 2)
        third(1, False, 0)
        pl.when(middle)(third_last)

        @pl.loop(1, DEFER_AT // 2)
        def _(p):
            third(2 * p, False, 2)
            third(2 * p + 1, False, 0)

        @pl.loop(DEFER_AT, last - 1)
        def _(c):
            third(c, False, 1)

        pl.when(jnp.logical_not(middle))(third_last)
        exchanged(last - 1, 1)
    else:
        third(0, True, 1)

        @pl.loop(1, last)
        def _(c):
            third(c, False, 1)

        exchanged(last, 1)

    wait(y.at[:, :, pl.ds(0, hw * (wide - 1)), :], ws_sem.at[0])
    wait(z.at[:, :, pl.ds(0, hn * (narrow - 1)), :], ns_sem.at[0])


def finish(c, done, arrived, left, out, value, sem):
    slabs, order = done.shape[1], done.shape[2]
    others = [i for i in range(slabs) if i != c]

    def write(i):
        return pltpu.make_async_copy(done.at[:, i], out.at[:, i], sem.at[0])

    for i in others:
        write(i).start()
    high, low = split(arrived[c].reshape(2 * order, order))
    stacked = jnp.concatenate([high, high, low], axis=0)
    value[...] = jnp.dot(left[2], stacked, preferred_element_type=F32).reshape(2, order, order)
    write_last = pltpu.make_async_copy(value, out.at[:, c], sem.at[1])
    write_last.start()
    for i in others:
        write(i).wait()
    write_last.wait()


def fused(wide, narrow, amplitudes, gates):
    layout = amplitudes.shape
    slabs, order = layout[1], layout[4]
    vector = amplitudes.reshape(2, slabs, order, order)
    matrices = gates.reshape(6, 2, order, order)
    early = narrow == 4 and slabs == 8
    slots = slabs + early
    slab_buffer = pltpu.VMEM((slots, 2, order, order), F32)
    done, arrived, left = pl.pallas_call(
        functools.partial(kernel, wide, narrow, early),
        out_shape=[
            jax.ShapeDtypeStruct(vector.shape, F32),
            jax.ShapeDtypeStruct((slabs, 2, order, order), F32),
            jax.ShapeDtypeStruct((3, 2 * order, 6 * order), BF16),
        ],
        in_specs=[pl.BlockSpec(memory_space=pl.ANY)] * 2,
        out_specs=[pl.BlockSpec(memory_space=pltpu.VMEM)] * 3,
        scratch_shapes=[
            pltpu.VMEM((2, slots, order, order), F32),
            pltpu.VMEM(matrices.shape, F32),
            slab_buffer, slab_buffer, slab_buffer,
            pltpu.VMEM((6 * order, 2 * order), BF16),
            pltpu.SemaphoreType.REGULAR((5,)),
            pltpu.SemaphoreType.DMA((5,)),
            pltpu.SemaphoreType.DMA((1,)),
            pltpu.SemaphoreType.DMA((slabs,)),
            pltpu.SemaphoreType.DMA((1,)),
            pltpu.SemaphoreType.DMA((slabs - 1 - DEFER_AT // 2 if early else slabs,)),
            pltpu.SemaphoreType.DMA((1 + early,)),
        ],
        compiler_params=pltpu.CompilerParams(
            collective_id=0, has_side_effects=True, vmem_limit_bytes=24 << 20),
    )(*[pltpu.with_memory_space_constraint(value, pltpu.HBM) for value in (vector, matrices)])
    result = pl.pallas_call(
        functools.partial(finish, slabs - 1 - early),
        out_shape=jax.ShapeDtypeStruct(vector.shape, F32),
        in_specs=[pl.BlockSpec(memory_space=pltpu.VMEM)] * 3,
        out_specs=pl.BlockSpec(memory_space=pltpu.HBM),
        scratch_shapes=[
            pltpu.VMEM((2, order, order), F32),
            pltpu.SemaphoreType.DMA((2,)),
        ],
        compiler_params=pltpu.CompilerParams(vmem_limit_bytes=8 << 20),
    )(done, arrived, left)
    return result.reshape(layout)


def tiled(order, count):
    return count > 1 and count & (count - 1) == 0 and order % (8 * count) == 0


def solution(mesh):
    wide, narrow = mesh.shape["wide"], mesh.shape["narrow"]

    def shards(amplitudes, gates):
        order, slabs = amplitudes.shape[4], amplitudes.shape[1]
        if tiled(order, wide) and tiled(order, narrow) and wide * narrow <= 128 and slabs > 2:
            return fused(wide, narrow, amplitudes, gates)
        return plain(amplitudes, gates)

    return jax.shard_map(
        shards,
        mesh=mesh,
        in_specs=(P(None, None, "wide", "narrow", None, None), P()),
        out_specs=P(None, None, "wide", "narrow", None, None),
        check_vma=False,
    )
```
